32 devices in a mesh: groups: 2 (over y), chan: 4 (over z), tm: 2 (over x), sub: 2 (over core).
Axes of the slice: x: 2, y: 2, z: 4, core: 2. Of those that a mesh axis runs over, the one named last changes fastest.
Arguments:
- traces: float32 [2048, 8192], P(('groups', 'chan', 'sub'), 'tm'), parts along dimension 0, may hold values from -6 to 6
- filters: float32 [2048, 65], P(('groups', 'chan', 'sub')), parts along dimension 0, may hold values from -0.75 to 0.75
- sources: int32 [256], P('groups'), parts along dimension 0, may hold values from 0 to 1023, as said below
Outputs:
- corr: float32 [128, 129, 2048], P('tm', None, ('groups', 'chan', 'sub')), parts along dimension 2
The draws below stay inside these ranges and needn't reach their ends.
There are 2 independent parts, one for each index of `groups`. The reference program is written for one: setup_inputs(seed, part) draws one part's arguments, and reference() takes and returns one part's arrays. A program takes and returns all parts, laid end to end along the dimension named above; each array names one. Nothing has to cross between parts.
Inputs may be any that keep to these rules, and one draw needn't show every extreme that they name: `sources`: the 128 partner channels are distinct. No block of 128 consecutive channels starting at a multiple of 128 holds more than 16 of them, and some block holds exactly 16.
All inputs are finite; a program needn't handle non-finite values.
Results may differ from the reference program's by a relative error of at most 0.0033.
Values may be sent and summed in bfloat16 or wider, within the bound.
A program may use at most 64 MiB of HBM per device.

```python
import math
import jax
import jax.numpy as jnp
from jax import lax

C = 1024
P_SIZE = 128
TAPS = 65
LAGS = 129
CB = 128
MOST = 16
SAMPLES = 8192


def draw_sources(key, part):
    blocks = C // CB
    key_head, key_order, key_prefer, key_noise, key_shuffle = jax.random.split(jax.random.fold_in(key, 17), 5)
    head_block = jax.random.randint(key_head, (), 0, blocks)
    order_scores = jax.random.randint(key_order, (blocks, CB), 0, 65536) * CB + jnp.arange(CB, dtype=jnp.int32)[None, :]
    within = jnp.argsort(order_scores, axis=1, stable=True)[:, :MOST]
    slot_chan = jnp.arange(blocks, dtype=jnp.int32)[:, None] * CB + within
    prefer = jax.random.randint(key_prefer, (blocks, 1), 0, 4)
    noise_part = jax.random.randint(key_noise, (blocks, MOST), 0, 2048)
    slot_index = jnp.arange(blocks * MOST, dtype=jnp.int32).reshape(blocks, MOST)
    scores = (prefer * 2048 + noise_part) * (blocks * MOST) + slot_index
    is_head = jnp.arange(blocks, dtype=jnp.int32)[:, None] == head_block
    scores = jnp.where(is_head, 8192 * blocks * MOST + slot_index, scores)
    top_values, chosen = lax.top_k(scores.reshape(-1), P_SIZE)
    picked = slot_chan.reshape(-1)[chosen]
    shuffle = jax.random.randint(key_shuffle, (P_SIZE,), 0, 65536) * P_SIZE + jnp.arange(P_SIZE, dtype=jnp.int32)
    return picked[jnp.argsort(shuffle, stable=True)].astype(jnp.int32)


def levels(stream_key, shape, cuts, least, high):
    loudness, own = 1.0, jax.random.fold_in(stream_key, 6)
    for position, blocks in cuts:
        draws = jnp.exp(jax.random.uniform(jax.random.fold_in(own, position), (blocks,), jnp.float32, least / len(cuts), high / len(cuts)))
        loudness = loudness * jnp.repeat(draws, shape[position] // blocks).reshape([-1 if axis == position else 1 for axis in range(len(shape))])
    return loudness


def noise(own_key, dims, width, reach, pieces=(), kind=jnp.bfloat16):
    level = levels(own_key, dims, pieces, -0.22, 0.18) if pieces else 1.0
    drawn = jax.random.normal(own_key, dims, jnp.float32) * width * level
    return jnp.minimum(jnp.maximum(drawn, -reach), reach).astype(kind)


def setup_inputs(seed: int = 0, part: int = 0) -> dict:
    key_of = jax.random.split(jax.random.key(seed), 4)
    part_keys = jax.random.split(jax.random.fold_in(key_of[3], part), 4)
    traces = noise(part_keys[0], (C, SAMPLES), 1.0, 6.0, ((0, 8), (1, 2)), jnp.float32)
    filters = noise(part_keys[1], (C, TAPS), TAPS ** -0.5, 0.75, ((0, 8),), jnp.float32)
    sources = draw_sources(jax.random.fold_in(jax.random.fold_in(key_of[3], part), 71), part)
    return dict(traces=traces, filters=filters, sources=sources)


def reference(traces, filters, sources):
    num_samples = traces.shape[1]
    half_taps = (TAPS - 1) // 2
    extended = jnp.pad(traces, ((0, 0), (half_taps, half_taps)))
    running = jnp.zeros(traces.shape, jnp.float32)
    for k in range(TAPS):
        running = running + filters[:, k:k + 1] * extended[:, k:k + num_samples]
    whitened = running.astype(jnp.bfloat16)
    partner_traces = whitened[sources]
    half_lags = (LAGS - 1) // 2
    padded = jnp.pad(whitened.astype(jnp.float32), ((0, 0), (half_lags, half_lags)))
    partner_float = partner_traces.astype(jnp.float32)

    def one_lag(lag_index):
        first_col = (LAGS - 1 - lag_index).astype(jnp.int32)
        shifted = lax.dynamic_slice_in_dim(padded, first_col, num_samples, 1)
        return jnp.dot(partner_float, shifted.T, precision=lax.Precision.HIGHEST)
    stacked = lax.map(one_lag, jnp.arange(LAGS, dtype=jnp.int32))
    norm_scale = 1.0 / math.sqrt(SAMPLES)
    return jnp.transpose(stacked, (1, 0, 2)) * norm_scale
```

```python
import functools
import math

import jax
import jax.numpy as jnp
from jax import lax
from jax.experimental import pallas as pl
from jax.experimental.pallas import tpu as pltpu
from jax.sharding import PartitionSpec as P

LAGS = 129
HALF = 64
EDGE = 128
LANES = 128
TB = 128
VMEM_LIMIT = 26 * 1024 * 1024


def filtered(xt, start, f_ref, taps):
    acc = jnp.zeros((TB, xt.shape[1]), jnp.float32)
    for r in range(8):
        part = None
        for m in range((taps - 1 - r) // 8 + 1):
            k = 8 * m + r
            term = f_ref[k : k + 1, :] * xt[pl.ds(start + 8 * m, TB + 8), :]
            part = term if part is None else part + term
        acc = acc + part[r : r + TB]
    return acc


def whiten_kernel(taps, x_ref, low_ref, high_ref, f_ref, pick_ref, w_ref, slot_ref, xt):
    seg = x_ref.shape[1]
    half_taps = (taps - 1) // 2
    lead = EDGE - half_taps
    xt[0:EDGE, :] = low_ref[...].T
    xt[seg + EDGE : seg + 2 * EDGE, :] = high_ref[...].T

    @pl.loop(0, seg // LANES)
    def _(b):
        t0 = pl.multiple_of(b * LANES, LANES)
        xt[pl.ds(t0 + EDGE, LANES), :] = x_ref[:, pl.ds(t0, LANES)].T

    @pl.loop(0, seg // TB)
    def _(b):
        t0 = pl.multiple_of(b * TB, TB)
        w = filtered(xt, t0 + lead, f_ref, taps).astype(jnp.bfloat16)
        w_ref[pl.ds(t0, TB), :] = w
        slot_ref[:, pl.ds(t0, TB)] = lax.dot_general(
            pick_ref[...], w, (((1,), (1,)), ((), ())), preferred_element_type=jnp.float32
        ).astype(jnp.bfloat16)


def whiten(x, low, high, filters_t, picker):
    chans, seg = x.shape
    slots = picker.shape[0]
    return pl.pallas_call(
        functools.partial(whiten_kernel, filters_t.shape[0]),
        out_shape=(
            jax.ShapeDtypeStruct((seg, chans), jnp.bfloat16),
            jax.ShapeDtypeStruct((slots, seg), jnp.bfloat16),
        ),
        in_specs=[pl.BlockSpec(memory_space=pltpu.VMEM)] * 5,
        out_specs=(pl.BlockSpec(memory_space=pltpu.VMEM),) * 2,
        scratch_shapes=[pltpu.VMEM((seg + 2 * EDGE, chans), jnp.float32)],
        compiler_params=pltpu.CompilerParams(vmem_limit_bytes=VMEM_LIMIT),
        name="whiten",
    )(x, low, high, filters_t, picker)


MESH = pl.DeviceIdType.MESH
CHUNKS = 4


def front_kernel(taps, sizes, x_ref, f_ref, pick_ref, w_ref, slot_ref, xt, low, high,
                 halo_send, halo_recv, w_send, w_recv, slot_send, slot_recv):
    peers, lines, subs = sizes
    seg = x_ref.shape[1]
    width = seg // CHUNKS
    half_taps = (taps - 1) // 2
    lead = EDGE - half_taps
    a, z, s = lax.axis_index("tm"), lax.axis_index("chan"), lax.axis_index("sub")
    other = lax.rem(a + 1, peers)
    twin = lax.rem(s + 1, subs)

    barrier = pltpu.get_barrier_semaphore()
    pl.semaphore_signal(barrier, inc=1, device_id={"tm": other}, device_id_type=MESH)
    pl.semaphore_signal(barrier, inc=1, device_id={"sub": twin}, device_id_type=MESH)
    for step in range(1, lines):
        pl.semaphore_signal(
            barrier, inc=1, device_id={"chan": lax.rem(z + step, lines)}, device_id_type=MESH
        )
    pl.semaphore_wait(barrier, lines + 1)

    def halo(side):
        src = x_ref.at[:, seg - EDGE : seg] if side == 0 else x_ref.at[:, 0:EDGE]
        return pltpu.make_async_remote_copy(
            src_ref=src, dst_ref=(low, high)[side], send_sem=halo_send.at[side],
            recv_sem=halo_recv.at[side], device_id={"tm": other}, device_id_type=MESH)

    halo(0).start()
    halo(1).start()

    def w_copy(q, part):
        view = w_ref.at[part, q * width : (q + 1) * width, :]
        return pltpu.make_async_remote_copy(
            src_ref=view, dst_ref=view, send_sem=w_send.at[q], recv_sem=w_recv.at[q],
            device_id={"tm": other}, device_id_type=MESH)

    def slot_copy(q, part, line, sub, lane, where):
        view = slot_ref.at[part, line, sub, :, q * width : (q + 1) * width]
        return pltpu.make_async_remote_copy(
            src_ref=view, dst_ref=view, send_sem=slot_send.at[q, lane],
            recv_sem=slot_recv.at[q, part, line, sub], device_id=where, device_id_type=MESH)

    def others():
        return [lax.rem(z + step, lines) for step in range(1, lines)]

    def spread(q, part, base):
        copies = [
            slot_copy(q, part, z, s, base + i, {"chan": line}) for i, line in enumerate(others())
        ]
        return copies + [slot_copy(q, part, z, s, base + lines - 1, {"sub": twin})]

    def first(q):
        return [slot_copy(q, a, z, s, 0, {"tm": other})] + spread(q, a, 1)

    def second(q):
        return spread(q, other, 1 + lines)

    def third(q):
        return [
            slot_copy(q, part, line, s, 1 + 2 * lines + i * (lines - 1) + j, {"sub": twin})
            for i, part in enumerate((a, other))
            for j, line in enumerate(others())
        ]

    def launch(copies):
        for copy in copies:
            copy.start()

    def stage_two(q):
        slot_copy(q, other, z, s, 0, {"tm": other}).wait_recv()
        launch(second(q))

    def stage_three(q):
        for part in (a, other):
            for line in others():
                slot_copy(q, part, line, s, 0, {"chan": line}).wait_recv()
        launch(third(q))

    @pl.loop(0, seg // LANES)
    def _(b):
        t0 = pl.multiple_of(b * LANES, LANES)
        xt[pl.ds(t0 + EDGE, LANES), :] = x_ref[:, pl.ds(t0, LANES)].T

    halo(0).wait_recv()
    halo(1).wait_recv()
    xt[0:EDGE, :] = jnp.where(a > 0, low[...], 0.0).T
    xt[seg + EDGE : seg + 2 * EDGE, :] = jnp.where(a < peers - 1, high[...], 0.0).T

    for q in range(CHUNKS):

        @pl.loop(0, width // TB)
        def _(b):
            t0 = pl.multiple_of(q * width + b * TB, TB)
            w_ref[a, pl.ds(t0, TB), :] = filtered(xt, t0 + lead, f_ref, taps).astype(jnp.bfloat16)

        slot_ref[a, z, s, :, q * width : (q + 1) * width] = lax.dot_general(
            pick_ref[...], w_ref[a, q * width : (q + 1) * width, :],
            (((1,), (1,)), ((), ())), preferred_element_type=jnp.float32,
        ).astype(jnp.bfloat16)
        launch(first(q))
        w_copy(q, a).start()
        if q >= 1:
            stage_two(q - 1)
        if q >= 2:
            stage_three(q - 2)
    stage_two(CHUNKS - 1)
    stage_three(CHUNKS - 2)
    stage_three(CHUNKS - 1)
    halo(0).wait_send()
    halo(1).wait_send()
    for q in range(CHUNKS):
        for part in (a, other):
            for line in [z] + others():
                slot_copy(q, part, line, twin, 0, {"sub": twin}).wait_recv()
        w_copy(q, other).wait_recv()
        w_copy(q, a).wait_send()
        for copy in first(q) + second(q) + third(q):
            copy.wait_send()


def front(x, filters_t, picker, sizes):
    chans, seg = x.shape
    peers, lines, subs = sizes
    slots = picker.shape[0]
    dma = pltpu.SemaphoreType.DMA
    return pl.pallas_call(
        functools.partial(front_kernel, filters_t.shape[0], sizes),
        out_shape=(
            jax.ShapeDtypeStruct((peers, seg, chans), jnp.bfloat16),
            jax.ShapeDtypeStruct((peers, lines, subs, slots, seg), jnp.bfloat16),
        ),
        in_specs=[pl.BlockSpec(memory_space=pltpu.VMEM)] * 3,
        out_specs=(pl.BlockSpec(memory_space=pltpu.VMEM),) * 2,
        scratch_shapes=[
            pltpu.VMEM((seg + 2 * EDGE, chans), jnp.float32),
            pltpu.VMEM((chans, EDGE), jnp.float32),
            pltpu.VMEM((chans, EDGE), jnp.float32),
            dma((2,)), dma((2,)), dma((CHUNKS,)), dma((CHUNKS,)),
            dma((CHUNKS, 1 + 2 * lines + 2 * (lines - 1))),
            dma((CHUNKS, peers, lines, subs)),
        ],
        compiler_params=pltpu.CompilerParams(
            vmem_limit_bytes=VMEM_LIMIT, collective_id=0, has_side_effects=True
        ),
        name="front",
    )(x, filters_t, picker)


def chunk_of(total):
    return max(d for d in range(256, 1025, 256) if total % d == 0)


GROUP = 13


def corr_kernel(scale, w_ref, slot_ref, sel_ref, out_ref, rhs, xp, acc):
    parts, seg, chans = w_ref.shape
    span = parts * seg
    rows = sel_ref.shape[0]
    total = rhs.shape[0]
    depth = chunk_of(total)
    rhs[span:total, 0:chans] = jnp.zeros((total - span, chans), jnp.bfloat16)
    rhs[0:HALF, chans:] = jnp.zeros((HALF, chans), jnp.bfloat16)
    rhs[span + HALF : total, chans:] = jnp.zeros((total - span - HALF, chans), jnp.bfloat16)
    xp[:, 0:EDGE] = jnp.zeros((rows, EDGE), jnp.bfloat16)
    xp[:, EDGE + span :] = jnp.zeros((rows, xp.shape[1] - EDGE - span), jnp.bfloat16)
    for part in range(parts):
        rhs[part * seg : (part + 1) * seg, 0:chans] = w_ref[part]
        rhs[HALF + part * seg : HALF + (part + 1) * seg, chans:] = w_ref[part]
        xp[:, EDGE + part * seg : EDGE + (part + 1) * seg] = jnp.dot(
            sel_ref[...], slot_ref[part], preferred_element_type=jnp.float32
        ).astype(jnp.bfloat16)
    acc[...] = jnp.zeros_like(acc)

    @pl.loop(0, total // depth)
    def _(kb):
        k0 = pl.multiple_of(kb * depth, 256)
        xw = xp[:, pl.ds(k0, depth + 128)]
        r = rhs[pl.ds(k0, depth), :]
        for g in range((HALF + 1) // GROUP):
            lhs = jnp.concatenate(
                [
                    pltpu.roll(xw, depth + LANES - HALF - i, 1)[:, :depth]
                    for i in range(g * GROUP, (g + 1) * GROUP)
                ],
                axis=0,
            )
            here = slice(g * GROUP * rows, (g + 1) * GROUP * rows)
            acc[here, :] += jnp.dot(lhs, r, preferred_element_type=jnp.float32)

    for i in range(HALF + 1):
        if i < HALF:
            out_ref[i] = acc[i * rows : (i + 1) * rows, 0:chans] * scale
        out_ref[i + HALF] = acc[i * rows : (i + 1) * rows, chans:] * scale


def correlate(w_full, slots, select, scale):
    parts, seg, chans = w_full.shape
    rows = select.shape[0]
    total = parts * seg + 256
    return pl.pallas_call(
        functools.partial(corr_kernel, scale),
        out_shape=jax.ShapeDtypeStruct((LAGS, rows, chans), jnp.float32),
        in_specs=[pl.BlockSpec(memory_space=pltpu.VMEM)] * 3,
        out_specs=pl.BlockSpec(memory_space=pltpu.VMEM),
        scratch_shapes=[
            pltpu.VMEM((total, 2 * chans), jnp.bfloat16),
            pltpu.VMEM((rows, total + 128), jnp.bfloat16),
            pltpu.VMEM(((HALF + 1) * rows, 2 * chans), jnp.float32),
        ],
        compiler_params=pltpu.CompilerParams(vmem_limit_bytes=VMEM_LIMIT),
        name="correlate",
    )(w_full, slots, select)


def routing(sources, chan_dev, wide):
    partner_count = sources.shape[0]
    my_block = lax.axis_index(("chan", "sub"))
    owners = sources // chan_dev
    within = sources % chan_dev
    is_mine = owners == my_block
    chan_ids = jnp.arange(wide, dtype=jnp.int32)
    slot_most = min(chan_dev, partner_count // 8)
    order_ids = jnp.arange(partner_count, dtype=jnp.int32)
    same_owner = owners[:, None] == owners[None, :]
    earlier = order_ids[None, :] < order_ids[:, None]
    rank_in = jnp.sum((same_owner & earlier).astype(jnp.int32), axis=1)
    choose = (
        (rank_in[None, :] == jnp.arange(slot_most, dtype=jnp.int32)[:, None]) & is_mine[None, :]
    ).astype(jnp.bfloat16)
    onehot = (within[:, None] == chan_ids[None, :]).astype(jnp.bfloat16)
    picker = jnp.dot(choose, onehot, preferred_element_type=jnp.float32).astype(jnp.bfloat16)
    return picker, owners * slot_most + rank_in


def on_device(traces, filters, sources):
    chan_dev, seg_len = traces.shape
    time_devs = lax.axis_size("tm")
    wide = -(-chan_dev // LANES) * LANES
    picker, slot_id = routing(sources, chan_dev, wide)
    if wide != chan_dev:
        traces = jnp.pad(traces, ((0, wide - chan_dev), (0, 0)))
        filters = jnp.pad(filters, ((0, wide - chan_dev), (0, 0)))
    rows = slot_id.shape[0] // time_devs
    mine = lax.dynamic_slice_in_dim(slot_id, lax.axis_index("tm") * rows, rows, 0)
    lines, subs = lax.axis_size("chan"), lax.axis_size("sub")
    slot_count = picker.shape[0] * lines * subs
    select = (mine[:, None] == jnp.arange(slot_count, dtype=jnp.int32)[None, :]).astype(jnp.bfloat16)
    scale = 1.0 / math.sqrt(seg_len * time_devs)
    if time_devs == 2 and subs == 2:
        w_full, slots = front(traces, filters.T, picker, (time_devs, lines, subs))
        slots = slots.reshape(time_devs, slot_count, seg_len)
        corr = correlate(w_full, slots, select, scale)
    else:
        forward = [(i, i + 1) for i in range(time_devs - 1)]
        backward = [(target, source) for source, target in forward]
        low = lax.ppermute(traces[:, seg_len - EDGE :], "tm", forward)
        high = lax.ppermute(traces[:, :EDGE], "tm", backward)
        w_t, slot_rows = whiten(traces, low, high, filters.T, picker)
        segment = lax.all_gather(slot_rows, ("chan", "sub"), axis=0, tiled=True)
        w_full = lax.all_gather(w_t, "tm", axis=0, tiled=True)
        every = (
            slot_id[:, None] == jnp.arange(slot_count, dtype=jnp.int32)[None, :]
        ).astype(jnp.bfloat16)
        partners = jnp.dot(every, segment, preferred_element_type=jnp.float32).astype(jnp.bfloat16)
        partners = lax.all_to_all(partners, "tm", split_axis=0, concat_axis=1, tiled=True)
        corr = correlate(
            w_full[None], partners[None], jnp.eye(rows, dtype=jnp.bfloat16), scale
        )
    return jnp.transpose(corr, (1, 0, 2))[:, :, :chan_dev]


def solution(mesh):
    return jax.shard_map(
        on_device,
        mesh=mesh,
        in_specs=(
            P(("groups", "chan", "sub"), "tm"),
            P(("groups", "chan", "sub"), None),
            P("groups"),
        ),
        out_specs=P("tm", None, ("groups", "chan", "sub")),
        check_vma=False,
    )
```

```python
import functools
import math

import jax
import jax.numpy as jnp
from jax import lax
from jax.experimental import pallas as pl
from jax.experimental.pallas import tpu as pltpu
from jax.sharding import PartitionSpec as P

LAGS = 129
HALF = 64
EDGE = 128
LANES = 128
TB = 128
VMEM_LIMIT = 60 * 1024 * 1024


def filtered(xt, start, f_ref, taps):
    acc = jnp.zeros((TB, xt.shape[1]), jnp.float32)
    for r in range(8):
        part = None
        for m in range((taps - 1 - r) // 8 + 1):
            k = 8 * m + r
            term = f_ref[k : k + 1, :] * xt[pl.ds(start + 8 * m, TB + 8), :]
            part = term if part is None else part + term
        acc = acc + part[r : r + TB]
    return acc


def whiten_kernel(taps, x_ref, low_ref, high_ref, f_ref, pick_ref, w_ref, slot_ref, xt):
    seg = x_ref.shape[1]
    half_taps = (taps - 1) // 2
    lead = EDGE - half_taps
    xt[0:EDGE, :] = low_ref[...].T
    xt[seg + EDGE : seg + 2 * EDGE, :] = high_ref[...].T

    @pl.loop(0, seg // LANES)
    def _(b):
        t0 = pl.multiple_of(b * LANES, LANES)
        xt[pl.ds(t0 + EDGE, LANES), :] = x_ref[:, pl.ds(t0, LANES)].T

    @pl.loop(0, seg // TB)
    def _(b):
        t0 = pl.multiple_of(b * TB, TB)
        w = filtered(xt, t0 + lead, f_ref, taps).astype(jnp.bfloat16)
        w_ref[pl.ds(t0, TB), :] = w
        slot_ref[:, pl.ds(t0, TB)] = lax.dot_general(
            pick_ref[...], w, (((1,), (1,)), ((), ())), preferred_element_type=jnp.float32
        ).astype(jnp.bfloat16)


def whiten(x, low, high, filters_t, picker):
    chans, seg = x.shape
    slots = picker.shape[0]
    return pl.pallas_call(
        functools.partial(whiten_kernel, filters_t.shape[0]),
        out_shape=(
            jax.ShapeDtypeStruct((seg, chans), jnp.bfloat16),
            jax.ShapeDtypeStruct((slots, seg), jnp.bfloat16),
        ),
        in_specs=[pl.BlockSpec(memory_space=pltpu.VMEM)] * 5,
        out_specs=(pl.BlockSpec(memory_space=pltpu.VMEM),) * 2,
        scratch_shapes=[pltpu.VMEM((seg + 2 * EDGE, chans), jnp.float32)],
        compiler_params=pltpu.CompilerParams(vmem_limit_bytes=VMEM_LIMIT),
        name="whiten",
    )(x, low, high, filters_t, picker)


MESH = pl.DeviceIdType.MESH
CHUNKS = 4
DEEP = 1024
GROUP = 13
FRONT_LIMIT = 26 * 1024 * 1024
REST_LIMIT = 16 * 1024 * 1024


def accumulated(w_ref, xp_ref, k0, depth, chosen):
    xw = xp_ref[:, pl.ds(k0, depth + LANES)]
    r = jnp.concatenate(
        [
            w_ref[pl.ds(pl.multiple_of(k0 + EDGE, EDGE), depth), :],
            w_ref[pl.ds(pl.multiple_of(k0 + EDGE - HALF, HALF), depth), :],
        ],
        axis=1,
    )
    for group in chosen:
        lhs = jnp.concatenate(
            [pltpu.roll(xw, depth + LANES - HALF - i, 1)[:, :depth] for i in group], axis=0
        )
        yield group, jnp.dot(lhs, r, preferred_element_type=jnp.float32)


def groups():
    return [range(g, g + GROUP) for g in range(0, HALF + 1, GROUP)]


def add_terms(w_ref, xp_ref, acc_ref, k0, depth):
    rows = xp_ref.shape[0]
    for group, term in accumulated(w_ref, xp_ref, k0, depth, groups()):
        acc_ref[group[0] * rows : (group[-1] + 1) * rows, :] += term


def routing_tables(src, block, rows, half, blocks, chan_dev, slot_most, wide):
    count = src.shape[1]
    across = jnp.broadcast_to(src, (count, count))
    down = across.T

    def owner_of(ids):
        owner = jnp.zeros(ids.shape, jnp.int32)
        for b in range(1, blocks):
            owner = owner + jnp.where(ids >= b * chan_dev, 1, 0)
        return owner

    own_across, own_down = owner_of(across), owner_of(down)
    p_down = lax.broadcasted_iota(jnp.int32, (count, count), 0)
    p_across = lax.broadcasted_iota(jnp.int32, (count, count), 1)
    same = own_across == own_down
    rank_down = jnp.sum(jnp.where(same & (p_across < p_down), 1.0, 0.0), axis=1, keepdims=True)
    rank_across = jnp.sum(jnp.where(same & (p_down < p_across), 1.0, 0.0), axis=0, keepdims=True)
    slot_ids = lax.broadcasted_iota(jnp.int32, (slot_most, count), 0).astype(jnp.float32)
    mine = own_across[0:slot_most] == block
    choose = jnp.where((slot_ids == rank_across) & mine, 1.0, 0.0).astype(jnp.bfloat16)
    chan_ids = lax.broadcasted_iota(jnp.int32, (count, wide), 1)
    within = down[:, 0:1] - own_down[:, 0:1] * chan_dev
    onehot = jnp.where(within == chan_ids, 1.0, 0.0).astype(jnp.bfloat16)
    picker = jnp.dot(choose, onehot, preferred_element_type=jnp.float32).astype(jnp.bfloat16)
    slot_down = own_down[:, 0:1].astype(jnp.float32) * slot_most + rank_down
    slot_count = blocks * slot_most
    slots = lax.broadcasted_iota(jnp.int32, (count, slot_count), 1).astype(jnp.float32)
    every = jnp.where(slot_down == slots, 1.0, 0.0)
    select = every[0:rows]
    for h in range(1, count // rows):
        select = jnp.where(half == h, every[h * rows : (h + 1) * rows], select)
    return picker, select.astype(jnp.bfloat16)


def front_kernel(taps, sizes, slot_most, x_ref, f_ref, src_ref, w_ref, xp_ref, acc_ref,
                 x_v, xt, low, high, slot_ref, pick_ref, sel_ref,
                 x_sem, halo_send, halo_recv, w_send, w_recv, slot_send, slot_recv):
    peers, lines, subs = sizes
    chans, seg = x_ref.shape
    span = peers * seg
    rows = xp_ref.shape[0]
    width = seg // CHUNKS
    half_taps = (taps - 1) // 2
    lead = EDGE - half_taps
    a, z, s = lax.axis_index("tm"), lax.axis_index("chan"), lax.axis_index("sub")
    other = lax.rem(a + 1, peers)
    twin = lax.rem(s + 1, subs)

    barrier = pltpu.get_barrier_semaphore()
    pl.semaphore_signal(barrier, inc=1, device_id={"tm": other}, device_id_type=MESH)
    pl.semaphore_signal(barrier, inc=1, device_id={"sub": twin}, device_id_type=MESH)
    for step in range(1, lines):
        pl.semaphore_signal(
            barrier, inc=1, device_id={"chan": lax.rem(z + step, lines)}, device_id_type=MESH
        )

    def x_copy(q):
        here = slice(q * width, (q + 1) * width)
        return pltpu.make_async_copy(x_ref.at[:, here], x_v.at[:, here], x_sem.at[q])

    for q in range(CHUNKS):
        x_copy(q).start()

    picker, select = routing_tables(
        src_ref[...], z * subs + s, rows, a, lines * subs, chans, slot_most, chans
    )
    pick_ref[...] = picker
    sel_ref[...] = select
    w_ref[0:EDGE, :] = jnp.zeros((EDGE, chans), jnp.bfloat16)
    w_ref[EDGE + span :, :] = jnp.zeros((w_ref.shape[0] - EDGE - span, chans), jnp.bfloat16)
    xp_ref[:, 0:EDGE] = jnp.zeros((rows, EDGE), jnp.bfloat16)
    xp_ref[:, EDGE + span :] = jnp.zeros((rows, xp_ref.shape[1] - EDGE - span), jnp.bfloat16)
    acc_ref[...] = jnp.zeros_like(acc_ref)

    pl.semaphore_wait(barrier, lines + 1)

    def halo(side):
        src = x_ref.at[:, seg - EDGE : seg] if side == 0 else x_ref.at[:, 0:EDGE]
        return pltpu.make_async_remote_copy(
            src_ref=src, dst_ref=(low, high)[side], send_sem=halo_send.at[side],
            recv_sem=halo_recv.at[side], device_id={"tm": other}, device_id_type=MESH)

    halo(0).start()
    halo(1).start()

    def place(part, q):
        return pl.multiple_of(EDGE + part * seg + q * width, EDGE)

    def w_copy(q, part):
        view = w_ref.at[pl.ds(place(part, q), width), :]
        return pltpu.make_async_remote_copy(
            src_ref=view, dst_ref=view, send_sem=w_send.at[q], recv_sem=w_recv.at[q],
            device_id={"tm": other}, device_id_type=MESH)

    def columns(q):
        return pl.ds(pl.multiple_of(q * width, LANES), width)

    def slot_copy(q, part, line, sub, lane, where):
        view = slot_ref.at[part, line, sub, :, columns(q)]
        return pltpu.make_async_remote_copy(
            src_ref=view, dst_ref=view, send_sem=slot_send.at[q, lane],
            recv_sem=slot_recv.at[q, part, line, sub], device_id=where, device_id_type=MESH)

    def others():
        return [lax.rem(z + step, lines) for step in range(1, lines)]

    def spread(q, part, base):
        copies = [
            slot_copy(q, part, z, s, base + i, {"chan": line}) for i, line in enumerate(others())
        ]
        return copies + [slot_copy(q, part, z, s, base + lines - 1, {"sub": twin})]

    def first(q):
        return [slot_copy(q, a, z, s, 0, {"tm": other})] + spread(q, a, 1)

    def second(q):
        return spread(q, other, 1 + lines)

    def third(q, part):
        base = 1 + 2 * lines + (0 if part is a else lines - 1)
        return [
            slot_copy(q, part, line, s, base + j, {"sub": twin})
            for j, line in enumerate(others())
        ]

    def launch(copies):
        for copy in copies:
            copy.start()

    def across_time(q):
        slot_copy(q, other, z, s, 0, {"tm": other}).wait_recv()
        launch(second(q))

    def to_twin(q, part):
        for line in others():
            slot_copy(q, part, line, s, 0, {"chan": line}).wait_recv()
        launch(third(q, part))

    def fill_partners(q, part):
        for line in [z] + others():
            slot_copy(q, part, line, twin, 0, {"sub": twin}).wait_recv()
        rows_in = slot_ref[part, :, :, :, columns(q)].reshape(-1, width)
        xp_ref[:, pl.ds(place(part, q), width)] = jnp.dot(
            sel_ref[...], rows_in, preferred_element_type=jnp.float32
        ).astype(jnp.bfloat16)

    def nth(j):
        return lax.rem(j + 1, CHUNKS)

    for q in range(CHUNKS):
        x_copy(q).wait()

        @pl.loop(0, width // LANES)
        def _(b):
            t0 = pl.multiple_of(q * width + b * LANES, LANES)
            xt[pl.ds(t0 + EDGE, LANES), :] = x_v[:, pl.ds(t0, LANES)].T

    @pl.loop(0, CHUNKS)
    def _(j):
        q = nth(j)

        @pl.when(j == CHUNKS - 2)
        def _():
            halo(0).wait_recv()
            halo(1).wait_recv()
            xt[0:EDGE, :] = jnp.where(a > 0, low[...], 0.0).T
            xt[seg + EDGE : seg + 2 * EDGE, :] = jnp.where(a < peers - 1, high[...], 0.0).T

        @pl.loop(0, width // TB)
        def _(b):
            t0 = pl.multiple_of(q * width + b * TB, TB)
            w_ref[pl.ds(pl.multiple_of(EDGE + a * seg + t0, TB), TB), :] = filtered(
                xt, t0 + lead, f_ref, taps
            ).astype(jnp.bfloat16)

        slot_ref[a, z, s, :, columns(q)] = lax.dot_general(
            pick_ref[...], w_ref[pl.ds(place(a, q), width), :],
            (((1,), (1,)), ((), ())), preferred_element_type=jnp.float32,
        ).astype(jnp.bfloat16)
        launch(first(q))
        w_copy(q, a).start()

        @pl.when(j >= 1)
        def _():
            to_twin(nth(j - 1), a)

    @pl.loop(0, CHUNKS - 1)
    def _(j):
        fill_partners(nth(j), a)

    near = a * (seg + 256)

    @pl.loop(0, CHUNKS)
    def _(j):
        deep = jnp.where(j < CHUNKS - 2, j + 2, CHUNKS - 1 - j)
        add_terms(w_ref, xp_ref, acc_ref, pl.multiple_of(near + deep * width, 256), width)
        across_time(nth(j))

        @pl.when(j == 0)
        def _():
            to_twin(nth(CHUNKS - 1), a)

        @pl.when(j == CHUNKS - 3)
        def _():
            fill_partners(nth(CHUNKS - 1), a)

        @pl.when(j >= 1)
        def _():
            to_twin(nth(j - 1), other)

    to_twin(nth(CHUNKS - 1), other)
    halo(0).wait_send()
    halo(1).wait_send()

    @pl.loop(0, CHUNKS)
    def _(j):
        q = nth(j)
        fill_partners(q, other)
        w_copy(q, other).wait_recv()
        w_copy(q, a).wait_send()
        for copy in first(q) + second(q) + third(q, a) + third(q, other):
            copy.wait_send()


def front(x, filters_t, sources, sizes, slot_most):
    chans, seg = x.shape
    peers, lines, subs = sizes
    rows = sources.shape[0] // peers
    total = peers * seg + 256
    dma = pltpu.SemaphoreType.DMA
    vmem = pl.BlockSpec(memory_space=pltpu.VMEM)
    return pl.pallas_call(
        functools.partial(front_kernel, filters_t.shape[0], sizes, slot_most),
        out_shape=(
            jax.ShapeDtypeStruct((total + EDGE, chans), jnp.bfloat16),
            jax.ShapeDtypeStruct((rows, total + LANES), jnp.bfloat16),
            jax.ShapeDtypeStruct(((HALF + 1) * rows, 2 * chans), jnp.float32),
        ),
        in_specs=[pl.BlockSpec(memory_space=pl.ANY), vmem, vmem],
        out_specs=(vmem,) * 3,
        scratch_shapes=[
            pltpu.VMEM((chans, seg), jnp.float32),
            pltpu.VMEM((seg + 2 * EDGE, chans), jnp.float32),
            pltpu.VMEM((chans, EDGE), jnp.float32),
            pltpu.VMEM((chans, EDGE), jnp.float32),
            pltpu.VMEM((peers, lines, subs, slot_most, seg), jnp.bfloat16),
            pltpu.VMEM((slot_most, chans), jnp.bfloat16),
            pltpu.VMEM((rows, lines * subs * slot_most), jnp.bfloat16),
            dma((CHUNKS,)), dma((2,)), dma((2,)), dma((CHUNKS,)), dma((CHUNKS,)),
            dma((CHUNKS, 1 + 2 * lines + 2 * (lines - 1))),
            dma((CHUNKS, peers, lines, subs)),
        ],
        compiler_params=pltpu.CompilerParams(
            vmem_limit_bytes=FRONT_LIMIT, collective_id=0, has_side_effects=True
        ),
        name="front",
    )(x, filters_t, sources.reshape(1, -1))


def rest_kernel(scale, seg, w_ref, xp_ref, acc_ref, out_ref, part, stage, sems):
    rows = xp_ref.shape[0]
    chans = w_ref.shape[1]
    far = (1 - lax.axis_index("tm")) * seg
    for group, term in accumulated(w_ref, xp_ref, pl.multiple_of(far, 256), 256, groups()):
        here = slice(group[0] * rows, (group[-1] + 1) * rows)
        part[here, :] = acc_ref[here, :] + term

    @pl.loop(0, seg // DEEP - 1)
    def _(b):
        add_terms(w_ref, xp_ref, part, pl.multiple_of(far + 256 + b * DEEP, 256), DEEP)

    last = pl.multiple_of(far + 256 + seg - DEEP, 256)
    copies = []
    for n, (group, term) in enumerate(accumulated(w_ref, xp_ref, last, DEEP, groups())):
        start = group[0]
        for i in group:
            here = slice((i - start) * rows, (i - start + 1) * rows)
            held = part[i * rows : (i + 1) * rows, :] + term[here]
            if i < HALF:
                stage[i] = held[:, 0:chans] * scale
            stage[i + HALF] = held[:, chans:] * scale
        for m, (low, high) in enumerate(
            ((start, min(group[-1] + 1, HALF)), (start + HALF, group[-1] + 1 + HALF))
        ):
            copy = pltpu.make_async_copy(
                stage.at[low:high], out_ref.at[low:high], sems.at[n, m]
            )
            copy.start()
            copies.append(copy)
    for copy in copies:
        copy.wait()


def rest(w_full, partners, terms, seg, scale):
    rows = partners.shape[0]
    chans = w_full.shape[1]
    vmem = pl.BlockSpec(memory_space=pltpu.VMEM)
    return pl.pallas_call(
        functools.partial(rest_kernel, scale, seg),
        out_shape=jax.ShapeDtypeStruct((LAGS, rows, chans), jnp.float32),
        in_specs=[vmem] * 3,
        out_specs=pl.BlockSpec(memory_space=pl.ANY),
        scratch_shapes=[
            pltpu.VMEM(terms.shape, jnp.float32),
            pltpu.VMEM((LAGS, rows, chans), jnp.float32),
            pltpu.SemaphoreType.DMA((len(groups()), 2)),
        ],
        compiler_params=pltpu.CompilerParams(vmem_limit_bytes=REST_LIMIT),
        name="rest",
    )(w_full, partners, terms)


def chunk_of(total):
    return max(d for d in range(256, 1025, 256) if total % d == 0)


def corr_kernel(scale, w_ref, slot_ref, sel_ref, out_ref, rhs, xp, acc):
    parts, seg, chans = w_ref.shape
    span = parts * seg
    rows = sel_ref.shape[0]
    total = rhs.shape[0]
    depth = chunk_of(total)
    rhs[span:total, 0:chans] = jnp.zeros((total - span, chans), jnp.bfloat16)
    rhs[0:HALF, chans:] = jnp.zeros((HALF, chans), jnp.bfloat16)
    rhs[span + HALF : total, chans:] = jnp.zeros((total - span - HALF, chans), jnp.bfloat16)
    xp[:, 0:EDGE] = jnp.zeros((rows, EDGE), jnp.bfloat16)
    xp[:, EDGE + span :] = jnp.zeros((rows, xp.shape[1] - EDGE - span), jnp.bfloat16)
    for part in range(parts):
        rhs[part * seg : (part + 1) * seg, 0:chans] = w_ref[part]
        rhs[HALF + part * seg : HALF + (part + 1) * seg, chans:] = w_ref[part]
        xp[:, EDGE + part * seg : EDGE + (part + 1) * seg] = jnp.dot(
            sel_ref[...], slot_ref[part], preferred_element_type=jnp.float32
        ).astype(jnp.bfloat16)
    acc[...] = jnp.zeros_like(acc)

    @pl.loop(0, total // depth)
    def _(kb):
        k0 = pl.multiple_of(kb * depth, 256)
        xw = xp[:, pl.ds(k0, depth + 128)]
        r = rhs[pl.ds(k0, depth), :]
        for g in range((HALF + 1) // GROUP):
            lhs = jnp.concatenate(
                [
                    pltpu.roll(xw, depth + LANES - HALF - i, 1)[:, :depth]
                    for i in range(g * GROUP, (g + 1) * GROUP)
                ],
                axis=0,
            )
            here = slice(g * GROUP * rows, (g + 1) * GROUP * rows)
            acc[here, :] += jnp.dot(lhs, r, preferred_element_type=jnp.float32)

    for i in range(HALF + 1):
        if i < HALF:
            out_ref[i] = acc[i * rows : (i + 1) * rows, 0:chans] * scale
        out_ref[i + HALF] = acc[i * rows : (i + 1) * rows, chans:] * scale


def correlate(w_full, slots, select, scale):
    parts, seg, chans = w_full.shape
    rows = select.shape[0]
    total = parts * seg + 256
    return pl.pallas_call(
        functools.partial(corr_kernel, scale),
        out_shape=jax.ShapeDtypeStruct((LAGS, rows, chans), jnp.float32),
        in_specs=[pl.BlockSpec(memory_space=pltpu.VMEM)] * 3,
        out_specs=pl.BlockSpec(memory_space=pltpu.VMEM),
        scratch_shapes=[
            pltpu.VMEM((total, 2 * chans), jnp.bfloat16),
            pltpu.VMEM((rows, total + 128), jnp.bfloat16),
            pltpu.VMEM(((HALF + 1) * rows, 2 * chans), jnp.float32),
        ],
        compiler_params=pltpu.CompilerParams(vmem_limit_bytes=VMEM_LIMIT),
        name="correlate",
    )(w_full, slots, select)


def routing(sources, chan_dev, wide):
    partner_count = sources.shape[0]
    my_block = lax.axis_index(("chan", "sub"))
    owners = sources // chan_dev
    within = sources % chan_dev
    is_mine = owners == my_block
    chan_ids = jnp.arange(wide, dtype=jnp.int32)
    slot_most = min(chan_dev, partner_count // 8)
    order_ids = jnp.arange(partner_count, dtype=jnp.int32)
    same_owner = owners[:, None] == owners[None, :]
    earlier = order_ids[None, :] < order_ids[:, None]
    rank_in = jnp.sum((same_owner & earlier).astype(jnp.int32), axis=1)
    choose = (
        (rank_in[None, :] == jnp.arange(slot_most, dtype=jnp.int32)[:, None]) & is_mine[None, :]
    ).astype(jnp.bfloat16)
    onehot = (within[:, None] == chan_ids[None, :]).astype(jnp.bfloat16)
    picker = jnp.dot(choose, onehot, preferred_element_type=jnp.float32).astype(jnp.bfloat16)
    return picker, owners * slot_most + rank_in


def on_device(traces, filters, sources):
    chan_dev, seg_len = traces.shape
    time_devs = lax.axis_size("tm")
    lines, subs = lax.axis_size("chan"), lax.axis_size("sub")
    scale = 1.0 / math.sqrt(seg_len * time_devs)
    if time_devs == 2 and subs == 2 and chan_dev == LANES and seg_len % (CHUNKS * DEEP) == 0:
        slot_most = min(chan_dev, sources.shape[0] // 8)
        w_full, partners, terms = front(
            traces, filters.T, sources, (time_devs, lines, subs), slot_most
        )
        return jnp.transpose(rest(w_full, partners, terms, seg_len, scale), (1, 0, 2))
    wide = -(-chan_dev // LANES) * LANES
    picker, slot_id = routing(sources, chan_dev, wide)
    if wide != chan_dev:
        traces = jnp.pad(traces, ((0, wide - chan_dev), (0, 0)))
        filters = jnp.pad(filters, ((0, wide - chan_dev), (0, 0)))
    rows = slot_id.shape[0] // time_devs
    slot_count = picker.shape[0] * lines * subs
    forward = [(i, i + 1) for i in range(time_devs - 1)]
    backward = [(target, source) for source, target in forward]
    low = lax.ppermute(traces[:, seg_len - EDGE :], "tm", forward)
    high = lax.ppermute(traces[:, :EDGE], "tm", backward)
    w_t, slot_rows = whiten(traces, low, high, filters.T, picker)
    segment = lax.all_gather(slot_rows, ("chan", "sub"), axis=0, tiled=True)
    w_full = lax.all_gather(w_t, "tm", axis=0, tiled=True)
    every = (
        slot_id[:, None] == jnp.arange(slot_count, dtype=jnp.int32)[None, :]
    ).astype(jnp.bfloat16)
    partners = jnp.dot(every, segment, preferred_element_type=jnp.float32).astype(jnp.bfloat16)
    partners = lax.all_to_all(partners, "tm", split_axis=0, concat_axis=1, tiled=True)
    corr = correlate(
        w_full[None], partners[None], jnp.eye(rows, dtype=jnp.bfloat16), scale
    )
    return jnp.transpose(corr, (1, 0, 2))[:, :, :chan_dev]


def solution(mesh):
    return jax.shard_map(
        on_device,
        mesh=mesh,
        in_specs=(
            P(("groups", "chan", "sub"), "tm"),
            P(("groups", "chan", "sub"), None),
            P("groups"),
        ),
        out_specs=P("tm", None, ("groups", "chan", "sub")),
        check_vma=False,
    )
```

```python
import functools
import math

import jax
import jax.numpy as jnp
from jax import lax
from jax.experimental import pallas as pl
from jax.experimental.pallas import tpu as pltpu
from jax.sharding import PartitionSpec as P

LAGS = 129
HALF = 64
EDGE = 128
LANES = 128
TB = 128
VMEM_LIMIT = 60 * 1024 * 1024


def filtered(xt, start, f_ref, taps):
    acc = jnp.zeros((TB, xt.shape[1]), jnp.float32)
    for r in range(8):
        part = None
        for m in range((taps - 1 - r) // 8 + 1):
            k = 8 * m + r
            term = f_ref[k : k + 1, :] * xt[pl.ds(start + 8 * m, TB + 8), :]
            part = term if part is None else part + term
        acc = acc + part[r : r + TB]
    return acc


def whiten_kernel(taps, x_ref, low_ref, high_ref, f_ref, pick_ref, w_ref, slot_ref, xt):
    seg = x_ref.shape[1]
    half_taps = (taps - 1) // 2
    lead = EDGE - half_taps
    xt[0:EDGE, :] = low_ref[...].T
    xt[seg + EDGE : seg + 2 * EDGE, :] = high_ref[...].T

    @pl.loop(0, seg // LANES)
    def _(b):
        t0 = pl.multiple_of(b * LANES, LANES)
        xt[pl.ds(t0 + EDGE, LANES), :] = x_ref[:, pl.ds(t0, LANES)].T

    @pl.loop(0, seg // TB)
    def _(b):
        t0 = pl.multiple_of(b * TB, TB)
        w = filtered(xt, t0 + lead, f_ref, taps).astype(jnp.bfloat16)
        w_ref[pl.ds(t0, TB), :] = w
        slot_ref[:, pl.ds(t0, TB)] = lax.dot_general(
            pick_ref[...], w, (((1,), (1,)), ((), ())), preferred_element_type=jnp.float32
        ).astype(jnp.bfloat16)


def whiten(x, low, high, filters_t, picker):
    chans, seg = x.shape
    slots = picker.shape[0]
    return pl.pallas_call(
        functools.partial(whiten_kernel, filters_t.shape[0]),
        out_shape=(
            jax.ShapeDtypeStruct((seg, chans), jnp.bfloat16),
            jax.ShapeDtypeStruct((slots, seg), jnp.bfloat16),
        ),
        in_specs=[pl.BlockSpec(memory_space=pltpu.VMEM)] * 5,
        out_specs=(pl.BlockSpec(memory_space=pltpu.VMEM),) * 2,
        scratch_shapes=[pltpu.VMEM((seg + 2 * EDGE, chans), jnp.float32)],
        compiler_params=pltpu.CompilerParams(vmem_limit_bytes=VMEM_LIMIT),
        name="whiten",
    )(x, low, high, filters_t, picker)


MESH = pl.DeviceIdType.MESH
CHUNKS = 4
GROUP = 13
FRONT_LIMIT = 26 * 1024 * 1024
REST_LIMIT = 16 * 1024 * 1024


def accumulated(w_ref, xp_ref, k0, depth, chosen):
    xw = xp_ref[:, pl.ds(k0, depth + LANES)]
    r = jnp.concatenate(
        [
            w_ref[pl.ds(pl.multiple_of(k0 + EDGE, EDGE), depth), :],
            w_ref[pl.ds(pl.multiple_of(k0 + EDGE - HALF, HALF), depth), :],
        ],
        axis=1,
    )
    for group in chosen:
        lhs = jnp.concatenate(
            [pltpu.roll(xw, depth + LANES - HALF - i, 1)[:, :depth] for i in group], axis=0
        )
        yield group, jnp.dot(lhs, r, preferred_element_type=jnp.float32)


def groups():
    return [range(g, g + GROUP) for g in range(0, HALF + 1, GROUP)]


def add_terms(w_ref, xp_ref, acc_ref, k0, depth):
    rows = xp_ref.shape[0]
    for group, term in accumulated(w_ref, xp_ref, k0, depth, groups()):
        acc_ref[group[0] * rows : (group[-1] + 1) * rows, :] += term


def routing_tables(src, block, rows, half, blocks, chan_dev, slot_most, wide):
    count = src.shape[1]
    across = jnp.broadcast_to(src, (count, count))
    down = across.T

    def owner_of(ids):
        owner = jnp.zeros(ids.shape, jnp.int32)
        for b in range(1, blocks):
            owner = owner + jnp.where(ids >= b * chan_dev, 1, 0)
        return owner

    own_across, own_down = owner_of(across), owner_of(down)
    p_down = lax.broadcasted_iota(jnp.int32, (count, count), 0)
    p_across = lax.broadcasted_iota(jnp.int32, (count, count), 1)
    same = own_across == own_down
    rank_down = jnp.sum(jnp.where(same & (p_across < p_down), 1.0, 0.0), axis=1, keepdims=True)
    rank_across = jnp.sum(jnp.where(same & (p_down < p_across), 1.0, 0.0), axis=0, keepdims=True)
    slot_ids = lax.broadcasted_iota(jnp.int32, (slot_most, count), 0).astype(jnp.float32)
    mine = own_across[0:slot_most] == block
    choose = jnp.where((slot_ids == rank_across) & mine, 1.0, 0.0).astype(jnp.bfloat16)
    chan_ids = lax.broadcasted_iota(jnp.int32, (count, wide), 1)
    within = down[:, 0:1] - own_down[:, 0:1] * chan_dev
    onehot = jnp.where(within == chan_ids, 1.0, 0.0).astype(jnp.bfloat16)
    picker = jnp.dot(choose, onehot, preferred_element_type=jnp.float32).astype(jnp.bfloat16)
    slot_down = own_down[:, 0:1].astype(jnp.float32) * slot_most + rank_down
    slot_count = blocks * slot_most
    slots = lax.broadcasted_iota(jnp.int32, (count, slot_count), 1).astype(jnp.float32)
    every = jnp.where(slot_down == slots, 1.0, 0.0)
    select = every[0:rows]
    for h in range(1, count // rows):
        select = jnp.where(half == h, every[h * rows : (h + 1) * rows], select)
    return picker, select.astype(jnp.bfloat16)


def front_kernel(taps, sizes, slot_most, x_ref, f_hbm, src_hbm, w_ref, xp_ref, acc_ref,
                 f_ref, src_ref, x_v, xt, low, high, slot_ref, pick_ref, sel_ref,
                 x_sem, in_sem, halo_send, halo_recv, w_send, w_recv, slot_send, slot_recv):
    peers, lines, subs = sizes
    chans, seg = x_ref.shape
    span = peers * seg
    rows = xp_ref.shape[0]
    width = seg // CHUNKS
    half_taps = (taps - 1) // 2
    lead = EDGE - half_taps
    a, z, s = lax.axis_index("tm"), lax.axis_index("chan"), lax.axis_index("sub")
    other = lax.rem(a + 1, peers)
    twin = lax.rem(s + 1, subs)

    barrier = pltpu.get_barrier_semaphore()
    pl.semaphore_signal(barrier, inc=1, device_id={"tm": other}, device_id_type=MESH)
    pl.semaphore_signal(barrier, inc=1, device_id={"sub": twin}, device_id_type=MESH)
    for step in range(1, lines):
        pl.semaphore_signal(
            barrier, inc=1, device_id={"chan": lax.rem(z + step, lines)}, device_id_type=MESH
        )

    def x_copy(q):
        here = slice(q * width, (q + 1) * width)
        return pltpu.make_async_copy(x_ref.at[:, here], x_v.at[:, here], x_sem.at[q])

    small = [
        pltpu.make_async_copy(src_hbm, src_ref, in_sem.at[0]),
        pltpu.make_async_copy(f_hbm, f_ref, in_sem.at[1]),
    ]
    for copy in small:
        copy.start()
    for q in range(CHUNKS):
        x_copy(q).start()
    w_ref[0:EDGE, :] = jnp.zeros((EDGE, chans), jnp.bfloat16)
    w_ref[EDGE + span :, :] = jnp.zeros((w_ref.shape[0] - EDGE - span, chans), jnp.bfloat16)
    xp_ref[:, 0:EDGE] = jnp.zeros((rows, EDGE), jnp.bfloat16)
    xp_ref[:, EDGE + span :] = jnp.zeros((rows, xp_ref.shape[1] - EDGE - span), jnp.bfloat16)
    acc_ref[...] = jnp.zeros_like(acc_ref)
    for copy in small:
        copy.wait()

    picker, select = routing_tables(
        src_ref[...], z * subs + s, rows, a, lines * subs, chans, slot_most, chans
    )
    pick_ref[...] = picker
    sel_ref[...] = select

    pl.semaphore_wait(barrier, lines + 1)

    def halo(side):
        src = x_ref.at[:, seg - EDGE : seg] if side == 0 else x_ref.at[:, 0:EDGE]
        return pltpu.make_async_remote_copy(
            src_ref=src, dst_ref=(low, high)[side], send_sem=halo_send.at[side],
            recv_sem=halo_recv.at[side], device_id={"tm": other}, device_id_type=MESH)

    halo(0).start()
    halo(1).start()

    def place(part, q):
        return pl.multiple_of(EDGE + part * seg + q * width, EDGE)

    def w_copy(q, part):
        view = w_ref.at[pl.ds(place(part, q), width), :]
        return pltpu.make_async_remote_copy(
            src_ref=view, dst_ref=view, send_sem=w_send.at[q], recv_sem=w_recv.at[q],
            device_id={"tm": other}, device_id_type=MESH)

    def columns(q):
        return pl.ds(pl.multiple_of(q * width, LANES), width)

    def slot_copy(q, part, line, sub, lane, where):
        view = slot_ref.at[part, line, sub, :, columns(q)]
        return pltpu.make_async_remote_copy(
            src_ref=view, dst_ref=view, send_sem=slot_send.at[q, lane],
            recv_sem=slot_recv.at[q, part, line, sub], device_id=where, device_id_type=MESH)

    def others():
        return [lax.rem(z + step, lines) for step in range(1, lines)]

    def spread(q, part, base):
        copies = [
            slot_copy(q, part, z, s, base + i, {"chan": line}) for i, line in enumerate(others())
        ]
        return copies + [slot_copy(q, part, z, s, base + lines - 1, {"sub": twin})]

    def first(q):
        return [slot_copy(q, a, z, s, 0, {"tm": other})] + spread(q, a, 1)

    def second(q):
        return spread(q, other, 1 + lines)

    def third(q, part):
        base = 1 + 2 * lines + (0 if part is a else lines - 1)
        return [
            slot_copy(q, part, line, s, base + j, {"sub": twin})
            for j, line in enumerate(others())
        ]

    def launch(copies):
        for copy in copies:
            copy.start()

    def across_time(q):
        slot_copy(q, other, z, s, 0, {"tm": other}).wait_recv()
        launch(second(q))

    def to_twin(q, part):
        for line in others():
            slot_copy(q, part, line, s, 0, {"chan": line}).wait_recv()
        launch(third(q, part))

    def fill_partners(q, part):
        for line in [z] + others():
            slot_copy(q, part, line, twin, 0, {"sub": twin}).wait_recv()
        rows_in = slot_ref[part, :, :, :, columns(q)].reshape(-1, width)
        xp_ref[:, pl.ds(place(part, q), width)] = jnp.dot(
            sel_ref[...], rows_in, preferred_element_type=jnp.float32
        ).astype(jnp.bfloat16)

    final = CHUNKS - 1

    def nth(j):
        return jnp.where(j >= final, j, lax.rem(j + 1, final))

    for q in range(CHUNKS):
        x_copy(q).wait()

        @pl.loop(0, width // LANES)
        def _(b):
            t0 = pl.multiple_of(q * width + b * LANES, LANES)
            xt[pl.ds(t0 + EDGE, LANES), :] = x_v[:, pl.ds(t0, LANES)].T

    @pl.loop(0, CHUNKS)
    def _(j):
        q = nth(j)

        @pl.when(j == CHUNKS - 2)
        def _():
            halo(0).wait_recv()
            halo(1).wait_recv()
            xt[0:EDGE, :] = jnp.where(a > 0, low[...], 0.0).T
            xt[seg + EDGE : seg + 2 * EDGE, :] = jnp.where(a < peers - 1, high[...], 0.0).T

        @pl.loop(0, width // TB)
        def _(b):
            t0 = pl.multiple_of(q * width + b * TB, TB)
            w_ref[pl.ds(pl.multiple_of(EDGE + a * seg + t0, TB), TB), :] = filtered(
                xt, t0 + lead, f_ref, taps
            ).astype(jnp.bfloat16)

        slot_ref[a, z, s, :, columns(q)] = lax.dot_general(
            pick_ref[...], w_ref[pl.ds(place(a, q), width), :],
            (((1,), (1,)), ((), ())), preferred_element_type=jnp.float32,
        ).astype(jnp.bfloat16)
        launch(first(q))

        @pl.when((j == 0) | (j == final))
        def _():
            w_copy(nth(jnp.where(j == 0, 0, final - 1)), a).start()

        @pl.when(j >= 2)
        def _():
            w_copy(nth(jnp.where(j == final, final, j - 1)), a).start()

        @pl.when(j >= 1)
        def _():
            to_twin(nth(j - 1), a)

    @pl.loop(0, CHUNKS - 1)
    def _(j):
        fill_partners(nth(j), a)

    near = a * (seg + 256)
    far = other * seg

    def add_chunk(base, q):
        add_terms(w_ref, xp_ref, acc_ref, pl.multiple_of(base + q * width, 256), width)

    @pl.loop(0, CHUNKS)
    def _(j):
        add_chunk(near, jnp.where(j < 2, 1 - j, j))

        @pl.when(j == 0)
        def _():
            across_time(nth(0))
            to_twin(nth(final), a)

        @pl.when(j < final)
        def _():
            across_time(nth(j + 1))

        @pl.when(j == 1)
        def _():
            fill_partners(nth(final), a)

        @pl.when(j >= 1)
        def _():
            to_twin(nth(j - 1), other)

    to_twin(nth(final), other)

    def arrive(j):
        q = nth(j)
        fill_partners(q, other)
        w_copy(q, other).wait_recv()

    arrive(0)

    @pl.loop(1, CHUNKS)
    def _(j):
        @pl.when(j < final)
        def _():
            arrive(j)

        add_chunk(far, CHUNKS - 1 - j)

    arrive(final)
    halo(0).wait_send()
    halo(1).wait_send()

    @pl.loop(0, CHUNKS)
    def _(j):
        q = nth(j)
        w_copy(q, a).wait_send()
        for copy in first(q) + second(q) + third(q, a) + third(q, other):
            copy.wait_send()


def front(x, filters_t, sources, sizes, slot_most):
    chans, seg = x.shape
    peers, lines, subs = sizes
    rows = sources.shape[0] // peers
    total = peers * seg + 256
    dma = pltpu.SemaphoreType.DMA
    vmem = pl.BlockSpec(memory_space=pltpu.VMEM)
    return pl.pallas_call(
        functools.partial(front_kernel, filters_t.shape[0], sizes, slot_most),
        out_shape=(
            jax.ShapeDtypeStruct((total + EDGE, chans), jnp.bfloat16),
            jax.ShapeDtypeStruct((rows, total + LANES), jnp.bfloat16),
            jax.ShapeDtypeStruct(((HALF + 1) * rows, 2 * chans), jnp.float32),
        ),
        in_specs=[pl.BlockSpec(memory_space=pltpu.HBM)] * 3,
        out_specs=(vmem,) * 3,
        scratch_shapes=[
            pltpu.VMEM(filters_t.shape, jnp.float32),
            pltpu.VMEM((1, sources.shape[0]), jnp.int32),
            pltpu.VMEM((chans, seg), jnp.float32),
            pltpu.VMEM((seg + 2 * EDGE, chans), jnp.float32),
            pltpu.VMEM((chans, EDGE), jnp.float32),
            pltpu.VMEM((chans, EDGE), jnp.float32),
            pltpu.VMEM((peers, lines, subs, slot_most, seg), jnp.bfloat16),
            pltpu.VMEM((slot_most, chans), jnp.bfloat16),
            pltpu.VMEM((rows, lines * subs * slot_most), jnp.bfloat16),
            dma((CHUNKS,)), dma((2,)), dma((2,)), dma((2,)), dma((CHUNKS,)), dma((CHUNKS,)),
            dma((CHUNKS, 1 + 2 * lines + 2 * (lines - 1))),
            dma((CHUNKS, peers, lines, subs)),
        ],
        compiler_params=pltpu.CompilerParams(
            vmem_limit_bytes=FRONT_LIMIT, collective_id=0, has_side_effects=True
        ),
        name="front",
    )(*(
        pltpu.with_memory_space_constraint(value, pltpu.HBM)
        for value in (x, filters_t, sources.reshape(1, -1))
    ))


def rest_kernel(scale, seg, w_ref, xp_ref, acc_ref, out_ref, stage, sems):
    rows = xp_ref.shape[0]
    chans = w_ref.shape[1]
    far = (1 - lax.axis_index("tm")) * seg
    width = seg // CHUNKS
    last = pl.multiple_of(far + seg - width, 256)
    copies = []
    for n, (group, term) in enumerate(accumulated(w_ref, xp_ref, last, width + 256, groups())):
        start = group[0]
        for i in group:
            here = slice((i - start) * rows, (i - start + 1) * rows)
            held = acc_ref[i * rows : (i + 1) * rows, :] + term[here]
            if i < HALF:
                stage[i] = held[:, 0:chans] * scale
            stage[i + HALF] = held[:, chans:] * scale
        for m, (low, high) in enumerate(
            ((start, min(group[-1] + 1, HALF)), (start + HALF, group[-1] + 1 + HALF))
        ):
            copy = pltpu.make_async_copy(
                stage.at[low:high], out_ref.at[low:high], sems.at[n, m]
            )
            copy.start()
            copies.append(copy)
    for copy in copies:
        copy.wait()


def rest(w_full, partners, terms, seg, scale):
    rows = partners.shape[0]
    chans = w_full.shape[1]
    vmem = pl.BlockSpec(memory_space=pltpu.VMEM)
    return pl.pallas_call(
        functools.partial(rest_kernel, scale, seg),
        out_shape=jax.ShapeDtypeStruct((LAGS, rows, chans), jnp.float32),
        in_specs=[vmem] * 3,
        out_specs=pl.BlockSpec(memory_space=pl.ANY),
        scratch_shapes=[
            pltpu.VMEM((LAGS, rows, chans), jnp.float32),
            pltpu.SemaphoreType.DMA((len(groups()), 2)),
        ],
        compiler_params=pltpu.CompilerParams(vmem_limit_bytes=REST_LIMIT),
        name="rest",
    )(w_full, partners, terms)


def chunk_of(total):
    return max(d for d in range(256, 1025, 256) if total % d == 0)


def corr_kernel(scale, w_ref, slot_ref, sel_ref, out_ref, rhs, xp, acc):
    parts, seg, chans = w_ref.shape
    span = parts * seg
    rows = sel_ref.shape[0]
    total = rhs.shape[0]
    depth = chunk_of(total)
    rhs[span:total, 0:chans] = jnp.zeros((total - span, chans), jnp.bfloat16)
    rhs[0:HALF, chans:] = jnp.zeros((HALF, chans), jnp.bfloat16)
    rhs[span + HALF : total, chans:] = jnp.zeros((total - span - HALF, chans), jnp.bfloat16)
    xp[:, 0:EDGE] = jnp.zeros((rows, EDGE), jnp.bfloat16)
    xp[:, EDGE + span :] = jnp.zeros((rows, xp.shape[1] - EDGE - span), jnp.bfloat16)
    for part in range(parts):
        rhs[part * seg : (part + 1) * seg, 0:chans] = w_ref[part]
        rhs[HALF + part * seg : HALF + (part + 1) * seg, chans:] = w_ref[part]
        xp[:, EDGE + part * seg : EDGE + (part + 1) * seg] = jnp.dot(
            sel_ref[...], slot_ref[part], preferred_element_type=jnp.float32
        ).astype(jnp.bfloat16)
    acc[...] = jnp.zeros_like(acc)

    @pl.loop(0, total // depth)
    def _(kb):
        k0 = pl.multiple_of(kb * depth, 256)
        xw = xp[:, pl.ds(k0, depth + 128)]
        r = rhs[pl.ds(k0, depth), :]
        for g in range((HALF + 1) // GROUP):
            lhs = jnp.concatenate(
                [
                    pltpu.roll(xw, depth + LANES - HALF - i, 1)[:, :depth]
                    for i in range(g * GROUP, (g + 1) * GROUP)
                ],
                axis=0,
            )
            here = slice(g * GROUP * rows, (g + 1) * GROUP * rows)
            acc[here, :] += jnp.dot(lhs, r, preferred_element_type=jnp.float32)

    for i in range(HALF + 1):
        if i < HALF:
            out_ref[i] = acc[i * rows : (i + 1) * rows, 0:chans] * scale
        out_ref[i + HALF] = acc[i * rows : (i + 1) * rows, chans:] * scale


def correlate(w_full, slots, select, scale):
    parts, seg, chans = w_full.shape
    rows = select.shape[0]
    total = parts * seg + 256
    return pl.pallas_call(
        functools.partial(corr_kernel, scale),
        out_shape=jax.ShapeDtypeStruct((LAGS, rows, chans), jnp.float32),
        in_specs=[pl.BlockSpec(memory_space=pltpu.VMEM)] * 3,
        out_specs=pl.BlockSpec(memory_space=pltpu.VMEM),
        scratch_shapes=[
            pltpu.VMEM((total, 2 * chans), jnp.bfloat16),
            pltpu.VMEM((rows, total + 128), jnp.bfloat16),
            pltpu.VMEM(((HALF + 1) * rows, 2 * chans), jnp.float32),
        ],
        compiler_params=pltpu.CompilerParams(vmem_limit_bytes=VMEM_LIMIT),
        name="correlate",
    )(w_full, slots, select)


def routing(sources, chan_dev, wide):
    partner_count = sources.shape[0]
    my_block = lax.axis_index(("chan", "sub"))
    owners = sources // chan_dev
    within = sources % chan_dev
    is_mine = owners == my_block
    chan_ids = jnp.arange(wide, dtype=jnp.int32)
    slot_most = min(chan_dev, partner_count // 8)
    order_ids = jnp.arange(partner_count, dtype=jnp.int32)
    same_owner = owners[:, None] == owners[None, :]
    earlier = order_ids[None, :] < order_ids[:, None]
    rank_in = jnp.sum((same_owner & earlier).astype(jnp.int32), axis=1)
    choose = (
        (rank_in[None, :] == jnp.arange(slot_most, dtype=jnp.int32)[:, None]) & is_mine[None, :]
    ).astype(jnp.bfloat16)
    onehot = (within[:, None] == chan_ids[None, :]).astype(jnp.bfloat16)
    picker = jnp.dot(choose, onehot, preferred_element_type=jnp.float32).astype(jnp.bfloat16)
    return picker, owners * slot_most + rank_in


def on_device(traces, filters, sources):
    chan_dev, seg_len = traces.shape
    time_devs = lax.axis_size("tm")
    lines, subs = lax.axis_size("chan"), lax.axis_size("sub")
    scale = 1.0 / math.sqrt(seg_len * time_devs)
    if time_devs == 2 and subs == 2 and chan_dev == LANES and seg_len % (CHUNKS * 256) == 0:
        slot_most = min(chan_dev, sources.shape[0] // 8)
        w_full, partners, terms = front(
            traces, filters.T, sources, (time_devs, lines, subs), slot_most
        )
        return jnp.transpose(rest(w_full, partners, terms, seg_len, scale), (1, 0, 2))
    wide = -(-chan_dev // LANES) * LANES
    picker, slot_id = routing(sources, chan_dev, wide)
    if wide != chan_dev:
        traces = jnp.pad(traces, ((0, wide - chan_dev), (0, 0)))
        filters = jnp.pad(filters, ((0, wide - chan_dev), (0, 0)))
    rows = slot_id.shape[0] // time_devs
    slot_count = picker.shape[0] * lines * subs
    forward = [(i, i + 1) for i in range(time_devs - 1)]
    backward = [(target, source) for source, target in forward]
    low = lax.ppermute(traces[:, seg_len - EDGE :], "tm", forward)
    high = lax.ppermute(traces[:, :EDGE], "tm", backward)
    w_t, slot_rows = whiten(traces, low, high, filters.T, picker)
    segment = lax.all_gather(slot_rows, ("chan", "sub"), axis=0, tiled=True)
    w_full = lax.all_gather(w_t, "tm", axis=0, tiled=True)
    every = (
        slot_id[:, None] == jnp.arange(slot_count, dtype=jnp.int32)[None, :]
    ).astype(jnp.bfloat16)
    partners = jnp.dot(every, segment, preferred_element_type=jnp.float32).astype(jnp.bfloat16)
    partners = lax.all_to_all(partners, "tm", split_axis=0, concat_axis=1, tiled=True)
    corr = correlate(
        w_full[None], partners[None], jnp.eye(rows, dtype=jnp.bfloat16), scale
    )
    return jnp.transpose(corr, (1, 0, 2))[:, :, :chan_dev]


def solution(mesh):
    return jax.shard_map(
        on_device,
        mesh=mesh,
        in_specs=(
            P(("groups", "chan", "sub"), "tm"),
            P(("groups", "chan", "sub"), None),
            P("groups"),
        ),
        out_specs=P("tm", None, ("groups", "chan", "sub")),
        check_vma=False,
    )
```

```python
import functools
import math

import jax
import jax.numpy as jnp
from jax import lax
from jax.experimental import pallas as pl
from jax.experimental.pallas import tpu as pltpu
from jax.sharding import PartitionSpec as P

LAGS = 129
HALF = 64
EDGE = 128
LANES = 128
TB = 128
VMEM_LIMIT = 60 * 1024 * 1024


def filtered(xt, start, f_ref, taps):
    acc = jnp.zeros((TB, xt.shape[1]), jnp.float32)
    for r in range(8):
        part = None
        for m in range((taps - 1 - r) // 8 + 1):
            k = 8 * m + r
            term = f_ref[k : k + 1, :] * xt[pl.ds(start + 8 * m, TB + 8), :]
            part = term if part is None else part + term
        acc = acc + part[r : r + TB]
    return acc


def whiten_kernel(taps, x_ref, low_ref, high_ref, f_ref, pick_ref, w_ref, slot_ref, xt):
    seg = x_ref.shape[1]
    half_taps = (taps - 1) // 2
    lead = EDGE - half_taps
    xt[0:EDGE, :] = low_ref[...].T
    xt[seg + EDGE : seg + 2 * EDGE, :] = high_ref[...].T

    @pl.loop(0, seg // LANES)
    def _(b):
        t0 = pl.multiple_of(b * LANES, LANES)
        xt[pl.ds(t0 + EDGE, LANES), :] = x_ref[:, pl.ds(t0, LANES)].T

    @pl.loop(0, seg // TB)
    def _(b):
        t0 = pl.multiple_of(b * TB, TB)
        w = filtered(xt, t0 + lead, f_ref, taps).astype(jnp.bfloat16)
        w_ref[pl.ds(t0, TB), :] = w
        slot_ref[:, pl.ds(t0, TB)] = lax.dot_general(
            pick_ref[...], w, (((1,), (1,)), ((), ())), preferred_element_type=jnp.float32
        ).astype(jnp.bfloat16)


def whiten(x, low, high, filters_t, picker):
    chans, seg = x.shape
    slots = picker.shape[0]
    return pl.pallas_call(
        functools.partial(whiten_kernel, filters_t.shape[0]),
        out_shape=(
            jax.ShapeDtypeStruct((seg, chans), jnp.bfloat16),
            jax.ShapeDtypeStruct((slots, seg), jnp.bfloat16),
        ),
        in_specs=[pl.BlockSpec(memory_space=pltpu.VMEM)] * 5,
        out_specs=(pl.BlockSpec(memory_space=pltpu.VMEM),) * 2,
        scratch_shapes=[pltpu.VMEM((seg + 2 * EDGE, chans), jnp.float32)],
        compiler_params=pltpu.CompilerParams(vmem_limit_bytes=VMEM_LIMIT),
        name="whiten",
    )(x, low, high, filters_t, picker)


MESH = pl.DeviceIdType.MESH
CHUNKS = 4
GROUP = 13
FRONT_LIMIT = 26 * 1024 * 1024
REST_LIMIT = 16 * 1024 * 1024


def accumulated(w_ref, xp_ref, k0, depth, chosen):
    xw = xp_ref[:, pl.ds(k0, depth + LANES)]
    r = jnp.concatenate(
        [
            w_ref[pl.ds(pl.multiple_of(k0 + EDGE, EDGE), depth), :],
            w_ref[pl.ds(pl.multiple_of(k0 + EDGE - HALF, HALF), depth), :],
        ],
        axis=1,
    )
    for group in chosen:
        lhs = jnp.concatenate(
            [pltpu.roll(xw, depth + LANES - HALF - i, 1)[:, :depth] for i in group], axis=0
        )
        yield group, jnp.dot(lhs, r, preferred_element_type=jnp.float32)


def groups():
    return [range(g, g + GROUP) for g in range(0, HALF + 1, GROUP)]


def add_terms(w_ref, xp_ref, acc_ref, k0, depth):
    rows = xp_ref.shape[0]
    for group, term in accumulated(w_ref, xp_ref, k0, depth, groups()):
        acc_ref[group[0] * rows : (group[-1] + 1) * rows, :] += term


def routing_tables(src, block, rows, half, blocks, chan_dev, slot_most, wide):
    count = src.shape[1]
    across = jnp.broadcast_to(src, (count, count))
    down = across.T

    def owner_of(ids):
        owner = jnp.zeros(ids.shape, jnp.int32)
        for b in range(1, blocks):
            owner = owner + jnp.where(ids >= b * chan_dev, 1, 0)
        return owner

    own_across, own_down = owner_of(across), owner_of(down)
    p_down = lax.broadcasted_iota(jnp.int32, (count, count), 0)
    p_across = lax.broadcasted_iota(jnp.int32, (count, count), 1)
    same = own_across == own_down
    rank_down = jnp.sum(jnp.where(same & (p_across < p_down), 1.0, 0.0), axis=1, keepdims=True)
    rank_across = jnp.sum(jnp.where(same & (p_down < p_across), 1.0, 0.0), axis=0, keepdims=True)
    slot_ids = lax.broadcasted_iota(jnp.int32, (slot_most, count), 0).astype(jnp.float32)
    mine = own_across[0:slot_most] == block
    choose = jnp.where((slot_ids == rank_across) & mine, 1.0, 0.0).astype(jnp.bfloat16)
    chan_ids = lax.broadcasted_iota(jnp.int32, (count, wide), 1)
    within = down[:, 0:1] - own_down[:, 0:1] * chan_dev
    onehot = jnp.where(within == chan_ids, 1.0, 0.0).astype(jnp.bfloat16)
    picker = jnp.dot(choose, onehot, preferred_element_type=jnp.float32).astype(jnp.bfloat16)
    slot_down = own_down[:, 0:1].astype(jnp.float32) * slot_most + rank_down
    slot_count = blocks * slot_most
    slots = lax.broadcasted_iota(jnp.int32, (count, slot_count), 1).astype(jnp.float32)
    every = jnp.where(slot_down == slots, 1.0, 0.0)
    select = every[0:rows]
    for h in range(1, count // rows):
        select = jnp.where(half == h, every[h * rows : (h + 1) * rows], select)
    return picker, select.astype(jnp.bfloat16)


def front_kernel(taps, sizes, slot_most, x_ref, f_hbm, src_hbm, w_ref, xp_ref, acc_ref,
                 f_ref, src_ref, x_v, xt, low, high, slot_ref, pick_ref, sel_ref,
                 x_sem, in_sem, halo_send, halo_recv, w_send, w_recv, slot_send, slot_recv):
    peers, lines, subs = sizes
    chans, seg = x_ref.shape
    span = peers * seg
    rows = xp_ref.shape[0]
    width = seg // CHUNKS
    half_taps = (taps - 1) // 2
    lead = EDGE - half_taps
    a, z, s = lax.axis_index("tm"), lax.axis_index("chan"), lax.axis_index("sub")
    other = lax.rem(a + 1, peers)
    twin = lax.rem(s + 1, subs)

    barrier = pltpu.get_barrier_semaphore()
    pl.semaphore_signal(barrier, inc=1, device_id={"tm": other}, device_id_type=MESH)
    pl.semaphore_signal(barrier, inc=1, device_id={"sub": twin}, device_id_type=MESH)
    for step in range(1, lines):
        pl.semaphore_signal(
            barrier, inc=1, device_id={"chan": lax.rem(z + step, lines)}, device_id_type=MESH
        )

    def x_copy(q):
        here = slice(q * width, (q + 1) * width)
        return pltpu.make_async_copy(x_ref.at[:, here], x_v.at[:, here], x_sem.at[q])

    small = [
        pltpu.make_async_copy(src_hbm, src_ref, in_sem.at[0]),
        pltpu.make_async_copy(f_hbm, f_ref, in_sem.at[1]),
    ]
    for copy in small:
        copy.start()
    for q in range(CHUNKS):
        x_copy(q).start()
    w_ref[0:EDGE, :] = jnp.zeros((EDGE, chans), jnp.bfloat16)
    w_ref[EDGE + span :, :] = jnp.zeros((w_ref.shape[0] - EDGE - span, chans), jnp.bfloat16)
    xp_ref[:, 0:EDGE] = jnp.zeros((rows, EDGE), jnp.bfloat16)
    xp_ref[:, EDGE + span :] = jnp.zeros((rows, xp_ref.shape[1] - EDGE - span), jnp.bfloat16)
    acc_ref[...] = jnp.zeros_like(acc_ref)
    for copy in small:
        copy.wait()

    picker, select = routing_tables(
        src_ref[...], z * subs + s, rows, a, lines * subs, chans, slot_most, chans
    )
    pick_ref[...] = picker
    sel_ref[...] = select

    def halo(side):
        src = x_ref.at[:, seg - EDGE : seg] if side == 0 else x_ref.at[:, 0:EDGE]
        return pltpu.make_async_remote_copy(
            src_ref=src, dst_ref=(low, high)[side], send_sem=halo_send.at[side],
            recv_sem=halo_recv.at[side], device_id={"tm": other}, device_id_type=MESH)

    def place(part, q):
        return pl.multiple_of(EDGE + part * seg + q * width, EDGE)

    def w_copy(q, part):
        view = w_ref.at[pl.ds(place(part, q), width), :]
        return pltpu.make_async_remote_copy(
            src_ref=view, dst_ref=view, send_sem=w_send.at[q], recv_sem=w_recv.at[q],
            device_id={"tm": other}, device_id_type=MESH)

    def columns(q):
        return pl.ds(pl.multiple_of(q * width, LANES), width)

    def slot_copy(q, part, line, sub, lane, where):
        view = slot_ref.at[part, line, sub, :, columns(q)]
        return pltpu.make_async_remote_copy(
            src_ref=view, dst_ref=view, send_sem=slot_send.at[q, lane],
            recv_sem=slot_recv.at[q, part, line, sub], device_id=where, device_id_type=MESH)

    def others():
        return [lax.rem(z + step, lines) for step in range(1, lines)]

    def spread(q, part, base):
        copies = [
            slot_copy(q, part, z, s, base + i, {"chan": line}) for i, line in enumerate(others())
        ]
        return copies + [slot_copy(q, part, z, s, base + lines - 1, {"sub": twin})]

    def first(q):
        return [slot_copy(q, a, z, s, 0, {"tm": other})] + spread(q, a, 1)

    def second(q):
        return spread(q, other, 1 + lines)

    def third(q, part):
        base = 1 + 2 * lines + (0 if part is a else lines - 1)
        return [
            slot_copy(q, part, line, s, base + j, {"sub": twin})
            for j, line in enumerate(others())
        ]

    def launch(copies):
        for copy in copies:
            copy.start()

    def across_time(q):
        slot_copy(q, other, z, s, 0, {"tm": other}).wait_recv()
        launch(second(q))

    def to_twin(q, part):
        for line in others():
            slot_copy(q, part, line, s, 0, {"chan": line}).wait_recv()
        launch(third(q, part))

    def fill_partners(q, part):
        for line in [z] + others():
            slot_copy(q, part, line, twin, 0, {"sub": twin}).wait_recv()
        rows_in = slot_ref[part, :, :, :, columns(q)].reshape(-1, width)
        xp_ref[:, pl.ds(place(part, q), width)] = jnp.dot(
            sel_ref[...], rows_in, preferred_element_type=jnp.float32
        ).astype(jnp.bfloat16)

    final = CHUNKS - 1

    def nth(j):
        return jnp.where(j >= final, j, lax.rem(j + 1, final))

    for q in range(CHUNKS):
        x_copy(q).wait()

        @pl.loop(0, width // LANES)
        def _(b):
            t0 = pl.multiple_of(q * width + b * LANES, LANES)
            xt[pl.ds(t0 + EDGE, LANES), :] = x_v[:, pl.ds(t0, LANES)].T

    def whiten_chunk(q):
        @pl.loop(0, width // TB)
        def _(b):
            t0 = pl.multiple_of(q * width + b * TB, TB)
            w_ref[pl.ds(pl.multiple_of(EDGE + a * seg + t0, TB), TB), :] = filtered(
                xt, t0 + lead, f_ref, taps
            ).astype(jnp.bfloat16)

        slot_ref[a, z, s, :, columns(q)] = lax.dot_general(
            pick_ref[...], w_ref[pl.ds(place(a, q), width), :],
            (((1,), (1,)), ((), ())), preferred_element_type=jnp.float32,
        ).astype(jnp.bfloat16)

    whiten_chunk(1)
    pl.semaphore_wait(barrier, lines + 1)
    halo(0).start()
    halo(1).start()
    launch(first(1))
    w_copy(1, a).start()

    @pl.loop(1, CHUNKS)
    def _(j):
        @pl.when(j == CHUNKS - 2)
        def _():
            halo(0).wait_recv()
            halo(1).wait_recv()
            xt[0:EDGE, :] = jnp.where(a > 0, low[...], 0.0).T
            xt[seg + EDGE : seg + 2 * EDGE, :] = jnp.where(a < peers - 1, high[...], 0.0).T

        whiten_chunk(nth(j))
        launch(first(nth(j)))

        @pl.when(j >= 2)
        def _():
            w_copy(nth(j - 1), a).start()
            to_twin(nth(j - 2), a)

    w_copy(nth(final), a).start()
    across_time(nth(0))
    to_twin(nth(final - 1), a)
    across_time(nth(1))

    @pl.loop(0, 2)
    def _(j):
        fill_partners(nth(j), a)

    near = a * (seg + 256)
    far = other * seg

    def add_chunk(base, q):
        add_terms(w_ref, xp_ref, acc_ref, pl.multiple_of(base + q * width, 256), width)

    @pl.loop(0, CHUNKS)
    def _(j):
        add_chunk(near, jnp.where(j < final - a, final - 1 - a - j, j))

        @pl.when(j == 0)
        def _():
            fill_partners(nth(final - 1), a)
            across_time(nth(final - 1))

        @pl.when(j == 1)
        def _():
            to_twin(nth(final), a)
            to_twin(nth(0), other)
            fill_partners(nth(final), a)

        @pl.when(j == 2)
        def _():
            to_twin(nth(1), other)
            across_time(nth(final))

    to_twin(nth(final - 1), other)

    def arrive(j):
        q = nth(j)
        fill_partners(q, other)
        w_copy(q, other).wait_recv()

    arrive(0)

    @pl.loop(1, CHUNKS)
    def _(j):
        @pl.when(j < final)
        def _():
            arrive(j)

        add_chunk(far, CHUNKS - 1 - j)

        @pl.when(j == 1)
        def _():
            to_twin(nth(final), other)

    arrive(final)
    halo(0).wait_send()
    halo(1).wait_send()

    @pl.loop(0, CHUNKS)
    def _(j):
        q = nth(j)
        w_copy(q, a).wait_send()
        for copy in first(q) + second(q) + third(q, a) + third(q, other):
            copy.wait_send()


def front(x, filters_t, sources, sizes, slot_most):
    chans, seg = x.shape
    peers, lines, subs = sizes
    rows = sources.shape[0] // peers
    total = peers * seg + 256
    dma = pltpu.SemaphoreType.DMA
    vmem = pl.BlockSpec(memory_space=pltpu.VMEM)
    return pl.pallas_call(
        functools.partial(front_kernel, filters_t.shape[0], sizes, slot_most),
        out_shape=(
            jax.ShapeDtypeStruct((total + EDGE, chans), jnp.bfloat16),
            jax.ShapeDtypeStruct((rows, total + LANES), jnp.bfloat16),
            jax.ShapeDtypeStruct(((HALF + 1) * rows, 2 * chans), jnp.float32),
        ),
        in_specs=[pl.BlockSpec(memory_space=pltpu.HBM)] * 3,
        out_specs=(vmem,) * 3,
        scratch_shapes=[
            pltpu.VMEM(filters_t.shape, jnp.float32),
            pltpu.VMEM((1, sources.shape[0]), jnp.int32),
            pltpu.VMEM((chans, seg), jnp.float32),
            pltpu.VMEM((seg + 2 * EDGE, chans), jnp.float32),
            pltpu.VMEM((chans, EDGE), jnp.float32),
            pltpu.VMEM((chans, EDGE), jnp.float32),
            pltpu.VMEM((peers, lines, subs, slot_most, seg), jnp.bfloat16),
            pltpu.VMEM((slot_most, chans), jnp.bfloat16),
            pltpu.VMEM((rows, lines * subs * slot_most), jnp.bfloat16),
            dma((CHUNKS,)), dma((2,)), dma((2,)), dma((2,)), dma((CHUNKS,)), dma((CHUNKS,)),
            dma((CHUNKS, 1 + 2 * lines + 2 * (lines - 1))),
            dma((CHUNKS, peers, lines, subs)),
        ],
        compiler_params=pltpu.CompilerParams(
            vmem_limit_bytes=FRONT_LIMIT, collective_id=0, has_side_effects=True
        ),
        name="front",
    )(*(
        pltpu.with_memory_space_constraint(value, pltpu.HBM)
        for value in (x, filters_t, sources.reshape(1, -1))
    ))


def rest_kernel(scale, seg, w_ref, xp_ref, acc_ref, out_ref, stage, sems):
    rows = xp_ref.shape[0]
    chans = w_ref.shape[1]
    far = (1 - lax.axis_index("tm")) * seg
    width = seg // CHUNKS
    last = pl.multiple_of(far + seg - width, 256)
    copies = []
    for n, (group, term) in enumerate(accumulated(w_ref, xp_ref, last, width + 256, groups())):
        start = group[0]
        for i in group:
            here = slice((i - start) * rows, (i - start + 1) * rows)
            held = acc_ref[i * rows : (i + 1) * rows, :] + term[here]
            if i < HALF:
                stage[i] = held[:, 0:chans] * scale
            stage[i + HALF] = held[:, chans:] * scale
        for m, (low, high) in enumerate(
            ((start, min(group[-1] + 1, HALF)), (start + HALF, group[-1] + 1 + HALF))
        ):
            copy = pltpu.make_async_copy(
                stage.at[low:high], out_ref.at[low:high], sems.at[n, m]
            )
            copy.start()
            copies.append(copy)
    for copy in copies:
        copy.wait()


def rest(w_full, partners, terms, seg, scale):
    rows = partners.shape[0]
    chans = w_full.shape[1]
    vmem = pl.BlockSpec(memory_space=pltpu.VMEM)
    return pl.pallas_call(
        functools.partial(rest_kernel, scale, seg),
        out_shape=jax.ShapeDtypeStruct((LAGS, rows, chans), jnp.float32),
        in_specs=[vmem] * 3,
        out_specs=pl.BlockSpec(memory_space=pl.ANY),
        scratch_shapes=[
            pltpu.VMEM((LAGS, rows, chans), jnp.float32),
            pltpu.SemaphoreType.DMA((len(groups()), 2)),
        ],
        compiler_params=pltpu.CompilerParams(vmem_limit_bytes=REST_LIMIT),
        name="rest",
    )(w_full, partners, terms)


def chunk_of(total):
    return max(d for d in range(256, 1025, 256) if total % d == 0)


def corr_kernel(scale, w_ref, slot_ref, sel_ref, out_ref, rhs, xp, acc):
    parts, seg, chans = w_ref.shape
    span = parts * seg
    rows = sel_ref.shape[0]
    total = rhs.shape[0]
    depth = chunk_of(total)
    rhs[span:total, 0:chans] = jnp.zeros((total - span, chans), jnp.bfloat16)
    rhs[0:HALF, chans:] = jnp.zeros((HALF, chans), jnp.bfloat16)
    rhs[span + HALF : total, chans:] = jnp.zeros((total - span - HALF, chans), jnp.bfloat16)
    xp[:, 0:EDGE] = jnp.zeros((rows, EDGE), jnp.bfloat16)
    xp[:, EDGE + span :] = jnp.zeros((rows, xp.shape[1] - EDGE - span), jnp.bfloat16)
    for part in range(parts):
        rhs[part * seg : (part + 1) * seg, 0:chans] = w_ref[part]
        rhs[HALF + part * seg : HALF + (part + 1) * seg, chans:] = w_ref[part]
        xp[:, EDGE + part * seg : EDGE + (part + 1) * seg] = jnp.dot(
            sel_ref[...], slot_ref[part], preferred_element_type=jnp.float32
        ).astype(jnp.bfloat16)
    acc[...] = jnp.zeros_like(acc)

    @pl.loop(0, total // depth)
    def _(kb):
        k0 = pl.multiple_of(kb * depth, 256)
        xw = xp[:, pl.ds(k0, depth + 128)]
        r = rhs[pl.ds(k0, depth), :]
        for g in range((HALF + 1) // GROUP):
            lhs = jnp.concatenate(
                [
                    pltpu.roll(xw, depth + LANES - HALF - i, 1)[:, :depth]
                    for i in range(g * GROUP, (g + 1) * GROUP)
                ],
                axis=0,
            )
            here = slice(g * GROUP * rows, (g + 1) * GROUP * rows)
            acc[here, :] += jnp.dot(lhs, r, preferred_element_type=jnp.float32)

    for i in range(HALF + 1):
        if i < HALF:
            out_ref[i] = acc[i * rows : (i + 1) * rows, 0:chans] * scale
        out_ref[i + HALF] = acc[i * rows : (i + 1) * rows, chans:] * scale


def correlate(w_full, slots, select, scale):
    parts, seg, chans = w_full.shape
    rows = select.shape[0]
    total = parts * seg + 256
    return pl.pallas_call(
        functools.partial(corr_kernel, scale),
        out_shape=jax.ShapeDtypeStruct((LAGS, rows, chans), jnp.float32),
        in_specs=[pl.BlockSpec(memory_space=pltpu.VMEM)] * 3,
        out_specs=pl.BlockSpec(memory_space=pltpu.VMEM),
        scratch_shapes=[
            pltpu.VMEM((total, 2 * chans), jnp.bfloat16),
            pltpu.VMEM((rows, total + 128), jnp.bfloat16),
            pltpu.VMEM(((HALF + 1) * rows, 2 * chans), jnp.float32),
        ],
        compiler_params=pltpu.CompilerParams(vmem_limit_bytes=VMEM_LIMIT),
        name="correlate",
    )(w_full, slots, select)


def routing(sources, chan_dev, wide):
    partner_count = sources.shape[0]
    my_block = lax.axis_index(("chan", "sub"))
    owners = sources // chan_dev
    within = sources % chan_dev
    is_mine = owners == my_block
    chan_ids = jnp.arange(wide, dtype=jnp.int32)
    slot_most = min(chan_dev, partner_count // 8)
    order_ids = jnp.arange(partner_count, dtype=jnp.int32)
    same_owner = owners[:, None] == owners[None, :]
    earlier = order_ids[None, :] < order_ids[:, None]
    rank_in = jnp.sum((same_owner & earlier).astype(jnp.int32), axis=1)
    choose = (
        (rank_in[None, :] == jnp.arange(slot_most, dtype=jnp.int32)[:, None]) & is_mine[None, :]
    ).astype(jnp.bfloat16)
    onehot = (within[:, None] == chan_ids[None, :]).astype(jnp.bfloat16)
    picker = jnp.dot(choose, onehot, preferred_element_type=jnp.float32).astype(jnp.bfloat16)
    return picker, owners * slot_most + rank_in


def on_device(traces, filters, sources):
    chan_dev, seg_len = traces.shape
    time_devs = lax.axis_size("tm")
    lines, subs = lax.axis_size("chan"), lax.axis_size("sub")
    scale = 1.0 / math.sqrt(seg_len * time_devs)
    if time_devs == 2 and subs == 2 and chan_dev == LANES and seg_len % (CHUNKS * 256) == 0:
        slot_most = min(chan_dev, sources.shape[0] // 8)
        w_full, partners, terms = front(
            traces, filters.T, sources, (time_devs, lines, subs), slot_most
        )
        return jnp.transpose(rest(w_full, partners, terms, seg_len, scale), (1, 0, 2))
    wide = -(-chan_dev // LANES) * LANES
    picker, slot_id = routing(sources, chan_dev, wide)
    if wide != chan_dev:
        traces = jnp.pad(traces, ((0, wide - chan_dev), (0, 0)))
        filters = jnp.pad(filters, ((0, wide - chan_dev), (0, 0)))
    rows = slot_id.shape[0] // time_devs
    slot_count = picker.shape[0] * lines * subs
    forward = [(i, i + 1) for i in range(time_devs - 1)]
    backward = [(target, source) for source, target in forward]
    low = lax.ppermute(traces[:, seg_len - EDGE :], "tm", forward)
    high = lax.ppermute(traces[:, :EDGE], "tm", backward)
    w_t, slot_rows = whiten(traces, low, high, filters.T, picker)
    segment = lax.all_gather(slot_rows, ("chan", "sub"), axis=0, tiled=True)
    w_full = lax.all_gather(w_t, "tm", axis=0, tiled=True)
    every = (
        slot_id[:, None] == jnp.arange(slot_count, dtype=jnp.int32)[None, :]
    ).astype(jnp.bfloat16)
    partners = jnp.dot(every, segment, preferred_element_type=jnp.float32).astype(jnp.bfloat16)
    partners = lax.all_to_all(partners, "tm", split_axis=0, concat_axis=1, tiled=True)
    corr = correlate(
        w_full[None], partners[None], jnp.eye(rows, dtype=jnp.bfloat16), scale
    )
    return jnp.transpose(corr, (1, 0, 2))[:, :, :chan_dev]


def solution(mesh):
    return jax.shard_map(
        on_device,
        mesh=mesh,
        in_specs=(
            P(("groups", "chan", "sub"), "tm"),
            P(("groups", "chan", "sub"), None),
            P("groups"),
        ),
        out_specs=P("tm", None, ("groups", "chan", "sub")),
        check_vma=False,
    )
```

```python
import functools
import math

import jax
import jax.numpy as jnp
from jax import lax
from jax.experimental import pallas as pl
from jax.experimental.pallas import tpu as pltpu
from jax.sharding import PartitionSpec as P

LAGS = 129
HALF = 64
EDGE = 128
LANES = 128
TB = 128
VMEM_LIMIT = 60 * 1024 * 1024


def filtered(xt, start, f_ref, taps):
    acc = jnp.zeros((TB, xt.shape[1]), jnp.float32)
    for r in range(8):
        part = None
        for m in range((taps - 1 - r) // 8 + 1):
            k = 8 * m + r
            term = f_ref[k : k + 1, :] * xt[pl.ds(start + 8 * m, TB + 8), :]
            part = term if part is None else part + term
        acc = acc + part[r : r + TB]
    return acc


def whiten_kernel(taps, x_ref, low_ref, high_ref, f_ref, pick_ref, w_ref, slot_ref, xt):
    seg = x_ref.shape[1]
    half_taps = (taps - 1) // 2
    lead = EDGE - half_taps
    xt[0:EDGE, :] = low_ref[...].T
    xt[seg + EDGE : seg + 2 * EDGE, :] = high_ref[...].T

    @pl.loop(0, seg // LANES)
    def _(b):
        t0 = pl.multiple_of(b * LANES, LANES)
        xt[pl.ds(t0 + EDGE, LANES), :] = x_ref[:, pl.ds(t0, LANES)].T

    @pl.loop(0, seg // TB)
    def _(b):
        t0 = pl.multiple_of(b * TB, TB)
        w = filtered(xt, t0 + lead, f_ref, taps).astype(jnp.bfloat16)
        w_ref[pl.ds(t0, TB), :] = w
        slot_ref[:, pl.ds(t0, TB)] = lax.dot_general(
            pick_ref[...], w, (((1,), (1,)), ((), ())), preferred_element_type=jnp.float32
        ).astype(jnp.bfloat16)


def whiten(x, low, high, filters_t, picker):
    chans, seg = x.shape
    slots = picker.shape[0]
    return pl.pallas_call(
        functools.partial(whiten_kernel, filters_t.shape[0]),
        out_shape=(
            jax.ShapeDtypeStruct((seg, chans), jnp.bfloat16),
            jax.ShapeDtypeStruct((slots, seg), jnp.bfloat16),
        ),
        in_specs=[pl.BlockSpec(memory_space=pltpu.VMEM)] * 5,
        out_specs=(pl.BlockSpec(memory_space=pltpu.VMEM),) * 2,
        scratch_shapes=[pltpu.VMEM((seg + 2 * EDGE, chans), jnp.float32)],
        compiler_params=pltpu.CompilerParams(vmem_limit_bytes=VMEM_LIMIT),
        name="whiten",
    )(x, low, high, filters_t, picker)


MESH = pl.DeviceIdType.MESH
CHUNKS = 4
GROUP = 13
FRONT_LIMIT = 26 * 1024 * 1024
REST_LIMIT = 16 * 1024 * 1024


def accumulated(w_ref, xp_ref, k0, depth, chosen):
    xw = xp_ref[:, pl.ds(k0, depth + LANES)]
    r = jnp.concatenate(
        [
            w_ref[pl.ds(pl.multiple_of(k0 + EDGE, EDGE), depth), :],
            w_ref[pl.ds(pl.multiple_of(k0 + EDGE - HALF, HALF), depth), :],
        ],
        axis=1,
    )
    for group in chosen:
        lhs = jnp.concatenate(
            [pltpu.roll(xw, depth + LANES - HALF - i, 1)[:, :depth] for i in group], axis=0
        )
        yield group, jnp.dot(lhs, r, preferred_element_type=jnp.float32)


def groups():
    return [range(g, g + GROUP) for g in range(0, HALF + 1, GROUP)]


def add_terms(w_ref, xp_ref, acc_ref, k0, depth):
    rows = xp_ref.shape[0]
    for group, term in accumulated(w_ref, xp_ref, k0, depth, groups()):
        acc_ref[group[0] * rows : (group[-1] + 1) * rows, :] += term


PAIRS = 128


def weighted(x_ref, start, weights, count):
    acc = None
    for m, weight in enumerate(weights):
        term = weight * x_ref[pl.ds(start + m, count), :]
        acc = term if acc is None else acc + term
    return acc


def filtered_pairs(phases, start, f_ref, g_ref, taps, odd_sum, both):
    even_x, odd_x, sum_x = phases
    halves = taps // 2
    odd_sum[...] = weighted(
        odd_x, start, [f_ref[2 * m + 1 : 2 * m + 2, :] for m in range(halves)], PAIRS + 8
    )
    even = weighted(even_x, start, [f_ref[2 * m : 2 * m + 1, :] for m in range(halves + 1)], PAIRS)
    both[pl.ds(0, PAIRS, stride=2), :] = even + odd_sum[0:PAIRS, :]
    mixed = weighted(sum_x, start, [g_ref[m : m + 1, :] for m in range(halves + 1)], PAIRS)
    both[pl.ds(1, PAIRS, stride=2), :] = mixed - (even + odd_sum[1 : PAIRS + 1, :])
    return both[...]


def routing_tables(src, block, rows, half, blocks, chan_dev, slot_most, wide):
    count = src.shape[1]
    across = jnp.broadcast_to(src, (count, count))
    down = across.T

    def owner_of(ids):
        owner = jnp.zeros(ids.shape, jnp.int32)
        for b in range(1, blocks):
            owner = owner + jnp.where(ids >= b * chan_dev, 1, 0)
        return owner

    own_across, own_down = owner_of(across), owner_of(down)
    p_down = lax.broadcasted_iota(jnp.int32, (count, count), 0)
    p_across = lax.broadcasted_iota(jnp.int32, (count, count), 1)
    same = own_across == own_down
    rank_down = jnp.sum(jnp.where(same & (p_across < p_down), 1.0, 0.0), axis=1, keepdims=True)
    rank_across = jnp.sum(jnp.where(same & (p_down < p_across), 1.0, 0.0), axis=0, keepdims=True)
    slot_ids = lax.broadcasted_iota(jnp.int32, (slot_most, count), 0).astype(jnp.float32)
    mine = own_across[0:slot_most] == block
    choose = jnp.where((slot_ids == rank_across) & mine, 1.0, 0.0).astype(jnp.bfloat16)
    chan_ids = lax.broadcasted_iota(jnp.int32, (count, wide), 1)
    within = down[:, 0:1] - own_down[:, 0:1] * chan_dev
    onehot = jnp.where(within == chan_ids, 1.0, 0.0).astype(jnp.bfloat16)
    picker = jnp.dot(choose, onehot, preferred_element_type=jnp.float32).astype(jnp.bfloat16)
    slot_down = own_down[:, 0:1].astype(jnp.float32) * slot_most + rank_down
    slot_count = blocks * slot_most
    slots = lax.broadcasted_iota(jnp.int32, (count, slot_count), 1).astype(jnp.float32)
    every = jnp.where(slot_down == slots, 1.0, 0.0)
    select = every[0:rows]
    for h in range(1, count // rows):
        select = jnp.where(half == h, every[h * rows : (h + 1) * rows], select)
    return picker, select.astype(jnp.bfloat16)


def front_kernel(taps, sizes, slot_most, x_ref, f_hbm, src_hbm, w_ref, xp_ref, acc_ref,
                 f_ref, src_ref, x_v, even_x, odd_x, sum_x, g_ref, odd_sum, both, xt, low, high, slot_ref, pick_ref, sel_ref,
                 x_sem, in_sem, halo_send, halo_recv, w_send, w_recv, slot_send, slot_recv):
    peers, lines, subs = sizes
    chans, seg = x_ref.shape
    span = peers * seg
    rows = xp_ref.shape[0]
    width = seg // CHUNKS
    half_taps = (taps - 1) // 2
    lead = EDGE - half_taps
    a, z, s = lax.axis_index("tm"), lax.axis_index("chan"), lax.axis_index("sub")
    other = lax.rem(a + 1, peers)
    twin = lax.rem(s + 1, subs)

    barrier = pltpu.get_barrier_semaphore()
    pl.semaphore_signal(barrier, inc=1, device_id={"tm": other}, device_id_type=MESH)
    pl.semaphore_signal(barrier, inc=1, device_id={"sub": twin}, device_id_type=MESH)
    for step in range(1, lines):
        pl.semaphore_signal(
            barrier, inc=1, device_id={"chan": lax.rem(z + step, lines)}, device_id_type=MESH
        )

    def split(row):
        here = pl.ds(pl.multiple_of(row // 2, 8), LANES // 2)
        even = xt[pl.ds(row, LANES // 2, stride=2), :]
        odd = xt[pl.ds(row + 1, LANES // 2, stride=2), :]
        even_x[here, :] = even
        odd_x[here, :] = odd
        sum_x[here, :] = even + odd

    def x_copy(q):
        here = slice(q * width, (q + 1) * width)
        return pltpu.make_async_copy(x_ref.at[:, here], x_v.at[:, here], x_sem.at[q])

    small = [
        pltpu.make_async_copy(src_hbm, src_ref, in_sem.at[0]),
        pltpu.make_async_copy(f_hbm, f_ref, in_sem.at[1]),
    ]
    for copy in small:
        copy.start()
    for q in range(CHUNKS):
        x_copy(q).start()
    w_ref[0:EDGE, :] = jnp.zeros((EDGE, chans), jnp.bfloat16)
    w_ref[EDGE + span :, :] = jnp.zeros((w_ref.shape[0] - EDGE - span, chans), jnp.bfloat16)
    xp_ref[:, 0:EDGE] = jnp.zeros((rows, EDGE), jnp.bfloat16)
    xp_ref[:, EDGE + span :] = jnp.zeros((rows, xp_ref.shape[1] - EDGE - span), jnp.bfloat16)
    acc_ref[...] = jnp.zeros_like(acc_ref)
    for copy in small:
        copy.wait()
    g_ref[0:1, :] = f_ref[0:1, :]
    g_ref[1 : taps // 2 + 1, :] = (
        f_ref[pl.ds(2, taps // 2, stride=2), :] + f_ref[pl.ds(1, taps // 2, stride=2), :]
    )

    picker, select = routing_tables(
        src_ref[...], z * subs + s, rows, a, lines * subs, chans, slot_most, chans
    )
    pick_ref[...] = picker
    sel_ref[...] = select

    def halo(side):
        src = x_ref.at[:, seg - EDGE : seg] if side == 0 else x_ref.at[:, 0:EDGE]
        return pltpu.make_async_remote_copy(
            src_ref=src, dst_ref=(low, high)[side], send_sem=halo_send.at[side],
            recv_sem=halo_recv.at[side], device_id={"tm": other}, device_id_type=MESH)

    def place(part, q):
        return pl.multiple_of(EDGE + part * seg + q * width, EDGE)

    def w_copy(q, part):
        view = w_ref.at[pl.ds(place(part, q), width), :]
        return pltpu.make_async_remote_copy(
            src_ref=view, dst_ref=view, send_sem=w_send.at[q], recv_sem=w_recv.at[q],
            device_id={"tm": other}, device_id_type=MESH)

    def columns(q):
        return pl.ds(pl.multiple_of(q * width, LANES), width)

    def slot_copy(q, part, line, sub, lane, where):
        view = slot_ref.at[part, line, sub, :, columns(q)]
        return pltpu.make_async_remote_copy(
            src_ref=view, dst_ref=view, send_sem=slot_send.at[q, lane],
            recv_sem=slot_recv.at[q, part, line, sub], device_id=where, device_id_type=MESH)

    def others():
        return [lax.rem(z + step, lines) for step in range(1, lines)]

    def spread(q, part, base):
        copies = [
            slot_copy(q, part, z, s, base + i, {"chan": line}) for i, line in enumerate(others())
        ]
        return copies + [slot_copy(q, part, z, s, base + lines - 1, {"sub": twin})]

    def first(q):
        return [slot_copy(q, a, z, s, 0, {"tm": other})] + spread(q, a, 1)

    def second(q):
        return spread(q, other, 1 + lines)

    def third(q, part):
        base = 1 + 2 * lines + (0 if part is a else lines - 1)
        return [
            slot_copy(q, part, line, s, base + j, {"sub": twin})
            for j, line in enumerate(others())
        ]

    def launch(copies):
        for copy in copies:
            copy.start()

    def across_time(q):
        slot_copy(q, other, z, s, 0, {"tm": other}).wait_recv()
        launch(second(q))

    def to_twin(q, part):
        for line in others():
            slot_copy(q, part, line, s, 0, {"chan": line}).wait_recv()
        launch(third(q, part))

    def fill_partners(q, part):
        for line in [z] + others():
            slot_copy(q, part, line, twin, 0, {"sub": twin}).wait_recv()
        rows_in = slot_ref[part, :, :, :, columns(q)].reshape(-1, width)
        xp_ref[:, pl.ds(place(part, q), width)] = jnp.dot(
            sel_ref[...], rows_in, preferred_element_type=jnp.float32
        ).astype(jnp.bfloat16)

    final = CHUNKS - 1

    def nth(j):
        return jnp.where(j >= final, j, lax.rem(j + 1, final))

    for q in range(CHUNKS):
        x_copy(q).wait()

        @pl.loop(0, width // LANES)
        def _(b):
            t0 = pl.multiple_of(q * width + b * LANES, LANES)
            xt[pl.ds(t0 + EDGE, LANES), :] = x_v[:, pl.ds(t0, LANES)].T
            split(t0 + EDGE)

    def whiten_chunk(q):
        @pl.loop(0, width // (2 * PAIRS))
        def _(b):
            t0 = pl.multiple_of(q * width + b * 2 * PAIRS, 2 * PAIRS)
            start = pl.multiple_of((t0 + lead) // 2, 8)
            w_ref[pl.ds(pl.multiple_of(EDGE + a * seg + t0, EDGE), 2 * PAIRS), :] = (
                filtered_pairs(
                    (even_x, odd_x, sum_x), start, f_ref, g_ref, taps, odd_sum, both
                ).astype(jnp.bfloat16)
            )

        slot_ref[a, z, s, :, columns(q)] = lax.dot_general(
            pick_ref[...], w_ref[pl.ds(place(a, q), width), :],
            (((1,), (1,)), ((), ())), preferred_element_type=jnp.float32,
        ).astype(jnp.bfloat16)

    whiten_chunk(1)
    pl.semaphore_wait(barrier, lines + 1)
    halo(0).start()
    halo(1).start()
    launch(first(1))
    w_copy(1, a).start()

    @pl.loop(1, CHUNKS)
    def _(j):
        @pl.when(j == CHUNKS - 2)
        def _():
            halo(0).wait_recv()
            halo(1).wait_recv()
            xt[0:EDGE, :] = jnp.where(a > 0, low[...], 0.0).T
            xt[seg + EDGE : seg + 2 * EDGE, :] = jnp.where(a < peers - 1, high[...], 0.0).T
            split(0)
            split(seg + EDGE)

        whiten_chunk(nth(j))
        launch(first(nth(j)))

        @pl.when(j >= 2)
        def _():
            w_copy(nth(j - 1), a).start()
            to_twin(nth(j - 2), a)

    w_copy(nth(final), a).start()
    across_time(nth(0))
    to_twin(nth(final - 1), a)
    across_time(nth(1))

    @pl.loop(0, 2)
    def _(j):
        fill_partners(nth(j), a)

    near = a * (seg + 256)
    far = other * seg

    def add_chunk(base, q):
        add_terms(w_ref, xp_ref, acc_ref, pl.multiple_of(base + q * width, 256), width)

    @pl.loop(0, CHUNKS)
    def _(j):
        add_chunk(near, jnp.where(j < final - a, final - 1 - a - j, j))

        @pl.when(j == 0)
        def _():
            fill_partners(nth(final - 1), a)
            across_time(nth(final - 1))

        @pl.when(j == 1)
        def _():
            to_twin(nth(final), a)
            to_twin(nth(0), other)
            fill_partners(nth(final), a)

        @pl.when(j == 2)
        def _():
            to_twin(nth(1), other)
            across_time(nth(final))

    to_twin(nth(final - 1), other)

    def arrive(j):
        q = nth(j)
        fill_partners(q, other)
        w_copy(q, other).wait_recv()

    arrive(0)

    @pl.loop(1, CHUNKS)
    def _(j):
        @pl.when(j < final)
        def _():
            arrive(j)

        add_chunk(far, CHUNKS - 1 - j)

        @pl.when(j == 1)
        def _():
            to_twin(nth(final), other)

    arrive(final)
    halo(0).wait_send()
    halo(1).wait_send()

    @pl.loop(0, CHUNKS)
    def _(j):
        q = nth(j)
        w_copy(q, a).wait_send()
        for copy in first(q) + second(q) + third(q, a) + third(q, other):
            copy.wait_send()


def front(x, filters_t, sources, sizes, slot_most):
    chans, seg = x.shape
    peers, lines, subs = sizes
    rows = sources.shape[0] // peers
    total = peers * seg + 256
    dma = pltpu.SemaphoreType.DMA
    vmem = pl.BlockSpec(memory_space=pltpu.VMEM)
    return pl.pallas_call(
        functools.partial(front_kernel, filters_t.shape[0], sizes, slot_most),
        out_shape=(
            jax.ShapeDtypeStruct((total + EDGE, chans), jnp.bfloat16),
            jax.ShapeDtypeStruct((rows, total + LANES), jnp.bfloat16),
            jax.ShapeDtypeStruct(((HALF + 1) * rows, 2 * chans), jnp.float32),
        ),
        in_specs=[pl.BlockSpec(memory_space=pltpu.HBM)] * 3,
        out_specs=(vmem,) * 3,
        scratch_shapes=[
            pltpu.VMEM(filters_t.shape, jnp.float32),
            pltpu.VMEM((1, sources.shape[0]), jnp.int32),
            pltpu.VMEM((chans, seg), jnp.float32),
            *[pltpu.VMEM((seg // 2 + EDGE + 8, chans), jnp.float32)] * 3,
            pltpu.VMEM((filters_t.shape[0] // 2 + 1, chans), jnp.float32),
            pltpu.VMEM((PAIRS + 8, chans), jnp.float32),
            pltpu.VMEM((2 * PAIRS, chans), jnp.float32),
            pltpu.VMEM((seg + 2 * EDGE, chans), jnp.float32),
            pltpu.VMEM((chans, EDGE), jnp.float32),
            pltpu.VMEM((chans, EDGE), jnp.float32),
            pltpu.VMEM((peers, lines, subs, slot_most, seg), jnp.bfloat16),
            pltpu.VMEM((slot_most, chans), jnp.bfloat16),
            pltpu.VMEM((rows, lines * subs * slot_most), jnp.bfloat16),
            dma((CHUNKS,)), dma((2,)), dma((2,)), dma((2,)), dma((CHUNKS,)), dma((CHUNKS,)),
            dma((CHUNKS, 1 + 2 * lines + 2 * (lines - 1))),
            dma((CHUNKS, peers, lines, subs)),
        ],
        compiler_params=pltpu.CompilerParams(
            vmem_limit_bytes=FRONT_LIMIT, collective_id=0, has_side_effects=True
        ),
        name="front",
    )(*(
        pltpu.with_memory_space_constraint(value, pltpu.HBM)
        for value in (x, filters_t, sources.reshape(1, -1))
    ))


def rest_kernel(scale, seg, w_ref, xp_ref, acc_ref, out_ref, stage, sems):
    rows = xp_ref.shape[0]
    chans = w_ref.shape[1]
    far = (1 - lax.axis_index("tm")) * seg
    width = seg // CHUNKS
    last = pl.multiple_of(far + seg - width, 256)
    copies = []
    for n, (group, term) in enumerate(accumulated(w_ref, xp_ref, last, width + 256, groups())):
        start = group[0]
        for i in group:
            here = slice((i - start) * rows, (i - start + 1) * rows)
            held = acc_ref[i * rows : (i + 1) * rows, :] + term[here]
            if i < HALF:
                stage[i] = held[:, 0:chans] * scale
            stage[i + HALF] = held[:, chans:] * scale
        for m, (low, high) in enumerate(
            ((start, min(group[-1] + 1, HALF)), (start + HALF, group[-1] + 1 + HALF))
        ):
            copy = pltpu.make_async_copy(
                stage.at[low:high], out_ref.at[low:high], sems.at[n, m]
            )
            copy.start()
            copies.append(copy)
    for copy in copies:
        copy.wait()


def rest(w_full, partners, terms, seg, scale):
    rows = partners.shape[0]
    chans = w_full.shape[1]
    vmem = pl.BlockSpec(memory_space=pltpu.VMEM)
    return pl.pallas_call(
        functools.partial(rest_kernel, scale, seg),
        out_shape=jax.ShapeDtypeStruct((LAGS, rows, chans), jnp.float32),
        in_specs=[vmem] * 3,
        out_specs=pl.BlockSpec(memory_space=pl.ANY),
        scratch_shapes=[
            pltpu.VMEM((LAGS, rows, chans), jnp.float32),
            pltpu.SemaphoreType.DMA((len(groups()), 2)),
        ],
        compiler_params=pltpu.CompilerParams(vmem_limit_bytes=REST_LIMIT),
        name="rest",
    )(w_full, partners, terms)


def chunk_of(total):
    return max(d for d in range(256, 1025, 256) if total % d == 0)


def corr_kernel(scale, w_ref, slot_ref, sel_ref, out_ref, rhs, xp, acc):
    parts, seg, chans = w_ref.shape
    span = parts * seg
    rows = sel_ref.shape[0]
    total = rhs.shape[0]
    depth = chunk_of(total)
    rhs[span:total, 0:chans] = jnp.zeros((total - span, chans), jnp.bfloat16)
    rhs[0:HALF, chans:] = jnp.zeros((HALF, chans), jnp.bfloat16)
    rhs[span + HALF : total, chans:] = jnp.zeros((total - span - HALF, chans), jnp.bfloat16)
    xp[:, 0:EDGE] = jnp.zeros((rows, EDGE), jnp.bfloat16)
    xp[:, EDGE + span :] = jnp.zeros((rows, xp.shape[1] - EDGE - span), jnp.bfloat16)
    for part in range(parts):
        rhs[part * seg : (part + 1) * seg, 0:chans] = w_ref[part]
        rhs[HALF + part * seg : HALF + (part + 1) * seg, chans:] = w_ref[part]
        xp[:, EDGE + part * seg : EDGE + (part + 1) * seg] = jnp.dot(
            sel_ref[...], slot_ref[part], preferred_element_type=jnp.float32
        ).astype(jnp.bfloat16)
    acc[...] = jnp.zeros_like(acc)

    @pl.loop(0, total // depth)
    def _(kb):
        k0 = pl.multiple_of(kb * depth, 256)
        xw = xp[:, pl.ds(k0, depth + 128)]
        r = rhs[pl.ds(k0, depth), :]
        for g in range((HALF + 1) // GROUP):
            lhs = jnp.concatenate(
                [
                    pltpu.roll(xw, depth + LANES - HALF - i, 1)[:, :depth]
                    for i in range(g * GROUP, (g + 1) * GROUP)
                ],
                axis=0,
            )
            here = slice(g * GROUP * rows, (g + 1) * GROUP * rows)
            acc[here, :] += jnp.dot(lhs, r, preferred_element_type=jnp.float32)

    for i in range(HALF + 1):
        if i < HALF:
            out_ref[i] = acc[i * rows : (i + 1) * rows, 0:chans] * scale
        out_ref[i + HALF] = acc[i * rows : (i + 1) * rows, chans:] * scale


def correlate(w_full, slots, select, scale):
    parts, seg, chans = w_full.shape
    rows = select.shape[0]
    total = parts * seg + 256
    return pl.pallas_call(
        functools.partial(corr_kernel, scale),
        out_shape=jax.ShapeDtypeStruct((LAGS, rows, chans), jnp.float32),
        in_specs=[pl.BlockSpec(memory_space=pltpu.VMEM)] * 3,
        out_specs=pl.BlockSpec(memory_space=pltpu.VMEM),
        scratch_shapes=[
            pltpu.VMEM((total, 2 * chans), jnp.bfloat16),
            pltpu.VMEM((rows, total + 128), jnp.bfloat16),
            pltpu.VMEM(((HALF + 1) * rows, 2 * chans), jnp.float32),
        ],
        compiler_params=pltpu.CompilerParams(vmem_limit_bytes=VMEM_LIMIT),
        name="correlate",
    )(w_full, slots, select)


def routing(sources, chan_dev, wide):
    partner_count = sources.shape[0]
    my_block = lax.axis_index(("chan", "sub"))
    owners = sources // chan_dev
    within = sources % chan_dev
    is_mine = owners == my_block
    chan_ids = jnp.arange(wide, dtype=jnp.int32)
    slot_most = min(chan_dev, partner_count // 8)
    order_ids = jnp.arange(partner_count, dtype=jnp.int32)
    same_owner = owners[:, None] == owners[None, :]
    earlier = order_ids[None, :] < order_ids[:, None]
    rank_in = jnp.sum((same_owner & earlier).astype(jnp.int32), axis=1)
    choose = (
        (rank_in[None, :] == jnp.arange(slot_most, dtype=jnp.int32)[:, None]) & is_mine[None, :]
    ).astype(jnp.bfloat16)
    onehot = (within[:, None] == chan_ids[None, :]).astype(jnp.bfloat16)
    picker = jnp.dot(choose, onehot, preferred_element_type=jnp.float32).astype(jnp.bfloat16)
    return picker, owners * slot_most + rank_in


def on_device(traces, filters, sources):
    chan_dev, seg_len = traces.shape
    time_devs = lax.axis_size("tm")
    lines, subs = lax.axis_size("chan"), lax.axis_size("sub")
    scale = 1.0 / math.sqrt(seg_len * time_devs)
    paired = filters.shape[1] % 32 == 1 and filters.shape[1] < 2 * LANES
    if time_devs == 2 and subs == 2 and chan_dev == LANES and seg_len % (CHUNKS * 256) == 0 and paired:
        slot_most = min(chan_dev, sources.shape[0] // 8)
        w_full, partners, terms = front(
            traces, filters.T, sources, (time_devs, lines, subs), slot_most
        )
        return jnp.transpose(rest(w_full, partners, terms, seg_len, scale), (1, 0, 2))
    wide = -(-chan_dev // LANES) * LANES
    picker, slot_id = routing(sources, chan_dev, wide)
    if wide != chan_dev:
        traces = jnp.pad(traces, ((0, wide - chan_dev), (0, 0)))
        filters = jnp.pad(filters, ((0, wide - chan_dev), (0, 0)))
    rows = slot_id.shape[0] // time_devs
    slot_count = picker.shape[0] * lines * subs
    forward = [(i, i + 1) for i in range(time_devs - 1)]
    backward = [(target, source) for source, target in forward]
    low = lax.ppermute(traces[:, seg_len - EDGE :], "tm", forward)
    high = lax.ppermute(traces[:, :EDGE], "tm", backward)
    w_t, slot_rows = whiten(traces, low, high, filters.T, picker)
    segment = lax.all_gather(slot_rows, ("chan", "sub"), axis=0, tiled=True)
    w_full = lax.all_gather(w_t, "tm", axis=0, tiled=True)
    every = (
        slot_id[:, None] == jnp.arange(slot_count, dtype=jnp.int32)[None, :]
    ).astype(jnp.bfloat16)
    partners = jnp.dot(every, segment, preferred_element_type=jnp.float32).astype(jnp.bfloat16)
    partners = lax.all_to_all(partners, "tm", split_axis=0, concat_axis=1, tiled=True)
    corr = correlate(
        w_full[None], partners[None], jnp.eye(rows, dtype=jnp.bfloat16), scale
    )
    return jnp.transpose(corr, (1, 0, 2))[:, :, :chan_dev]


def solution(mesh):
    return jax.shard_map(
        on_device,
        mesh=mesh,
        in_specs=(
            P(("groups", "chan", "sub"), "tm"),
            P(("groups", "chan", "sub"), None),
            P("groups"),
        ),
        out_specs=P("tm", None, ("groups", "chan", "sub")),
        check_vma=False,
    )
```

```python
import functools
import math

import jax
import jax.numpy as jnp
from jax import lax
from jax.experimental import pallas as pl
from jax.experimental.pallas import tpu as pltpu
from jax.sharding import PartitionSpec as P

LAGS = 129
HALF = 64
EDGE = 128
LANES = 128
TB = 128
VMEM_LIMIT = 60 * 1024 * 1024


def filtered(xt, start, f_ref, taps):
    acc = jnp.zeros((TB, xt.shape[1]), jnp.float32)
    for r in range(8):
        part = None
        for m in range((taps - 1 - r) // 8 + 1):
            k = 8 * m + r
            term = f_ref[k : k + 1, :] * xt[pl.ds(start + 8 * m, TB + 8), :]
            part = term if part is None else part + term
        acc = acc + part[r : r + TB]
    return acc


def whiten_kernel(taps, x_ref, low_ref, high_ref, f_ref, pick_ref, w_ref, slot_ref, xt):
    seg = x_ref.shape[1]
    half_taps = (taps - 1) // 2
    lead = EDGE - half_taps
    xt[0:EDGE, :] = low_ref[...].T
    xt[seg + EDGE : seg + 2 * EDGE, :] = high_ref[...].T

    @pl.loop(0, seg // LANES)
    def _(b):
        t0 = pl.multiple_of(b * LANES, LANES)
        xt[pl.ds(t0 + EDGE, LANES), :] = x_ref[:, pl.ds(t0, LANES)].T

    @pl.loop(0, seg // TB)
    def _(b):
        t0 = pl.multiple_of(b * TB, TB)
        w = filtered(xt, t0 + lead, f_ref, taps).astype(jnp.bfloat16)
        w_ref[pl.ds(t0, TB), :] = w
        slot_ref[:, pl.ds(t0, TB)] = lax.dot_general(
            pick_ref[...], w, (((1,), (1,)), ((), ())), preferred_element_type=jnp.float32
        ).astype(jnp.bfloat16)


def whiten(x, low, high, filters_t, picker):
    chans, seg = x.shape
    slots = picker.shape[0]
    return pl.pallas_call(
        functools.partial(whiten_kernel, filters_t.shape[0]),
        out_shape=(
            jax.ShapeDtypeStruct((seg, chans), jnp.bfloat16),
            jax.ShapeDtypeStruct((slots, seg), jnp.bfloat16),
        ),
        in_specs=[pl.BlockSpec(memory_space=pltpu.VMEM)] * 5,
        out_specs=(pl.BlockSpec(memory_space=pltpu.VMEM),) * 2,
        scratch_shapes=[pltpu.VMEM((seg + 2 * EDGE, chans), jnp.float32)],
        compiler_params=pltpu.CompilerParams(vmem_limit_bytes=VMEM_LIMIT),
        name="whiten",
    )(x, low, high, filters_t, picker)


MESH = pl.DeviceIdType.MESH
CHUNKS = 4
GROUP = 13
FRONT_LIMIT = 26 * 1024 * 1024
REST_LIMIT = 16 * 1024 * 1024


def accumulated(w_ref, xp_ref, k0, depth, chosen):
    xw = xp_ref[:, pl.ds(k0, depth + LANES)]
    r = jnp.concatenate(
        [
            w_ref[pl.ds(pl.multiple_of(k0 + EDGE, EDGE), depth), :],
            w_ref[pl.ds(pl.multiple_of(k0 + EDGE - HALF, HALF), depth), :],
        ],
        axis=1,
    )
    for group in chosen:
        lhs = jnp.concatenate(
            [pltpu.roll(xw, depth + LANES - HALF - i, 1)[:, :depth] for i in group], axis=0
        )
        yield group, jnp.dot(lhs, r, preferred_element_type=jnp.float32)


def groups():
    return [range(g, g + GROUP) for g in range(0, HALF + 1, GROUP)]


def add_terms(w_ref, xp_ref, acc_ref, k0, depth):
    rows = xp_ref.shape[0]
    for group, term in accumulated(w_ref, xp_ref, k0, depth, groups()):
        acc_ref[group[0] * rows : (group[-1] + 1) * rows, :] += term


PAIRS = 128


def weighted(x_ref, start, weights, count):
    acc = None
    for m, weight in enumerate(weights):
        term = weight * x_ref[pl.ds(start + m, count), :]
        acc = term if acc is None else acc + term
    return acc


def filtered_pairs(phases, start, f_ref, g_ref, taps, odd_sum, both):
    even_x, odd_x, sum_x = phases
    halves = taps // 2
    odd_sum[...] = weighted(
        odd_x, start, [f_ref[2 * m + 1 : 2 * m + 2, :] for m in range(halves)], PAIRS + 8
    )
    even = weighted(even_x, start, [f_ref[2 * m : 2 * m + 1, :] for m in range(halves + 1)], PAIRS)
    both[pl.ds(0, PAIRS, stride=2), :] = even + odd_sum[0:PAIRS, :]
    mixed = weighted(sum_x, start, [g_ref[m : m + 1, :] for m in range(halves + 1)], PAIRS)
    both[pl.ds(1, PAIRS, stride=2), :] = mixed - (even + odd_sum[1 : PAIRS + 1, :])
    return both[...]


def routing_tables(src, block, rows, half, blocks, chan_dev, slot_most, wide):
    count = src.shape[1]
    across = jnp.broadcast_to(src, (count, count))
    down = across.T

    def owner_of(ids):
        owner = jnp.zeros(ids.shape, jnp.int32)
        for b in range(1, blocks):
            owner = owner + jnp.where(ids >= b * chan_dev, 1, 0)
        return owner

    own_across, own_down = owner_of(across), owner_of(down)
    p_down = lax.broadcasted_iota(jnp.int32, (count, count), 0)
    p_across = lax.broadcasted_iota(jnp.int32, (count, count), 1)
    same = own_across == own_down
    rank_down = jnp.sum(jnp.where(same & (p_across < p_down), 1.0, 0.0), axis=1, keepdims=True)
    rank_across = jnp.sum(jnp.where(same & (p_down < p_across), 1.0, 0.0), axis=0, keepdims=True)
    slot_ids = lax.broadcasted_iota(jnp.int32, (slot_most, count), 0).astype(jnp.float32)
    mine = own_across[0:slot_most] == block
    choose = jnp.where((slot_ids == rank_across) & mine, 1.0, 0.0).astype(jnp.bfloat16)
    chan_ids = lax.broadcasted_iota(jnp.int32, (count, wide), 1)
    within = down[:, 0:1] - own_down[:, 0:1] * chan_dev
    onehot = jnp.where(within == chan_ids, 1.0, 0.0).astype(jnp.bfloat16)
    picker = jnp.dot(choose, onehot, preferred_element_type=jnp.float32).astype(jnp.bfloat16)
    slot_down = own_down[:, 0:1].astype(jnp.float32) * slot_most + rank_down
    slot_count = blocks * slot_most
    slots = lax.broadcasted_iota(jnp.int32, (count, slot_count), 1).astype(jnp.float32)
    every = jnp.where(slot_down == slots, 1.0, 0.0)
    select = every[0:rows]
    for h in range(1, count // rows):
        select = jnp.where(half == h, every[h * rows : (h + 1) * rows], select)
    return picker, select.astype(jnp.bfloat16)


def front_kernel(taps, sizes, slot_most, x_ref, f_hbm, src_hbm, w_ref, xp_ref, acc_ref,
                 f_ref, src_ref, x_v, even_x, odd_x, sum_x, g_ref, odd_sum, both, xt, low, high, slot_ref, pick_ref, sel_ref,
                 x_sem, in_sem, halo_send, halo_recv, w_send, w_recv, slot_send, slot_recv):
    peers, lines, subs = sizes
    chans, seg = x_ref.shape
    span = peers * seg
    rows = xp_ref.shape[0]
    width = seg // CHUNKS
    half_taps = (taps - 1) // 2
    lead = EDGE - half_taps
    a, z, s = lax.axis_index("tm"), lax.axis_index("chan"), lax.axis_index("sub")
    other = lax.rem(a + 1, peers)
    twin = lax.rem(s + 1, subs)

    barrier = pltpu.get_barrier_semaphore()
    pl.semaphore_signal(barrier, inc=1, device_id={"tm": other}, device_id_type=MESH)
    pl.semaphore_signal(barrier, inc=1, device_id={"sub": twin}, device_id_type=MESH)
    for step in range(1, lines):
        pl.semaphore_signal(
            barrier, inc=1, device_id={"chan": lax.rem(z + step, lines)}, device_id_type=MESH
        )

    def split(row):
        here = pl.ds(pl.multiple_of(row // 2, 8), LANES // 2)
        even = xt[pl.ds(row, LANES // 2, stride=2), :]
        odd = xt[pl.ds(row + 1, LANES // 2, stride=2), :]
        even_x[here, :] = even
        odd_x[here, :] = odd
        sum_x[here, :] = even + odd

    def x_copy(q):
        here = slice(q * width, (q + 1) * width)
        return pltpu.make_async_copy(x_ref.at[:, here], x_v.at[:, here], x_sem.at[q])

    small = [
        pltpu.make_async_copy(src_hbm, src_ref, in_sem.at[0]),
        pltpu.make_async_copy(f_hbm, f_ref, in_sem.at[1]),
    ]
    for copy in small:
        copy.start()
    for q in range(CHUNKS):
        x_copy(q).start()
    w_ref[0:EDGE, :] = jnp.zeros((EDGE, chans), jnp.bfloat16)
    w_ref[EDGE + span :, :] = jnp.zeros((w_ref.shape[0] - EDGE - span, chans), jnp.bfloat16)
    xp_ref[:, 0:EDGE] = jnp.zeros((rows, EDGE), jnp.bfloat16)
    xp_ref[:, EDGE + span :] = jnp.zeros((rows, xp_ref.shape[1] - EDGE - span), jnp.bfloat16)
    acc_ref[...] = jnp.zeros_like(acc_ref)
    for copy in small:
        copy.wait()
    g_ref[0:1, :] = f_ref[0:1, :]
    g_ref[1 : taps // 2 + 1, :] = (
        f_ref[pl.ds(2, taps // 2, stride=2), :] + f_ref[pl.ds(1, taps // 2, stride=2), :]
    )

    picker, select = routing_tables(
        src_ref[...], z * subs + s, rows, a, lines * subs, chans, slot_most, chans
    )
    pick_ref[...] = picker
    sel_ref[...] = select

    def halo(side):
        src = x_ref.at[:, seg - EDGE : seg] if side == 0 else x_ref.at[:, 0:EDGE]
        return pltpu.make_async_remote_copy(
            src_ref=src, dst_ref=(low, high)[side], send_sem=halo_send.at[side],
            recv_sem=halo_recv.at[side], device_id={"tm": other}, device_id_type=MESH)

    def place(part, q):
        return pl.multiple_of(EDGE + part * seg + q * width, EDGE)

    def w_copy(q, part):
        view = w_ref.at[pl.ds(place(part, q), width), :]
        return pltpu.make_async_remote_copy(
            src_ref=view, dst_ref=view, send_sem=w_send.at[q], recv_sem=w_recv.at[q],
            device_id={"tm": other}, device_id_type=MESH)

    def columns(q):
        return pl.ds(pl.multiple_of(q * width, LANES), width)

    def slot_copy(q, part, line, sub, lane, where):
        view = slot_ref.at[part, line, sub, :, columns(q)]
        return pltpu.make_async_remote_copy(
            src_ref=view, dst_ref=view, send_sem=slot_send.at[q, lane],
            recv_sem=slot_recv.at[q, part, line, sub], device_id=where, device_id_type=MESH)

    def others():
        return [lax.rem(z + step, lines) for step in range(1, lines)]

    def spread(q, part, base):
        copies = [
            slot_copy(q, part, z, s, base + i, {"chan": line}) for i, line in enumerate(others())
        ]
        return copies + [slot_copy(q, part, z, s, base + lines - 1, {"sub": twin})]

    def first(q):
        return [slot_copy(q, a, z, s, 0, {"tm": other})] + spread(q, a, 1)

    def second(q):
        return spread(q, other, 1 + lines)

    def third(q, part):
        base = 1 + 2 * lines + (0 if part is a else lines - 1)
        return [
            slot_copy(q, part, line, s, base + j, {"sub": twin})
            for j, line in enumerate(others())
        ]

    def launch(copies):
        for copy in copies:
            copy.start()

    def across_time(q):
        slot_copy(q, other, z, s, 0, {"tm": other}).wait_recv()
        launch(second(q))

    def to_twin(q, part):
        for line in others():
            slot_copy(q, part, line, s, 0, {"chan": line}).wait_recv()
        launch(third(q, part))

    def fill_partners(q, part):
        for line in [z] + others():
            slot_copy(q, part, line, twin, 0, {"sub": twin}).wait_recv()
        rows_in = slot_ref[part, :, :, :, columns(q)].reshape(-1, width)
        xp_ref[:, pl.ds(place(part, q), width)] = jnp.dot(
            sel_ref[...], rows_in, preferred_element_type=jnp.float32
        ).astype(jnp.bfloat16)

    final = CHUNKS - 1

    def nth(j):
        return jnp.where(j >= final, j, lax.rem(j + 1, final))

    for q in range(CHUNKS):
        x_copy(q).wait()

        @pl.loop(0, width // LANES)
        def _(b):
            t0 = pl.multiple_of(q * width + b * LANES, LANES)
            xt[pl.ds(t0 + EDGE, LANES), :] = x_v[:, pl.ds(t0, LANES)].T
            split(t0 + EDGE)

    def whiten_chunk(q):
        @pl.loop(0, width // (2 * PAIRS))
        def _(b):
            t0 = pl.multiple_of(q * width + b * 2 * PAIRS, 2 * PAIRS)
            start = pl.multiple_of((t0 + lead) // 2, 8)
            w_ref[pl.ds(pl.multiple_of(EDGE + a * seg + t0, EDGE), 2 * PAIRS), :] = (
                filtered_pairs(
                    (even_x, odd_x, sum_x), start, f_ref, g_ref, taps, odd_sum, both
                ).astype(jnp.bfloat16)
            )

        slot_ref[a, z, s, :, columns(q)] = lax.dot_general(
            pick_ref[...], w_ref[pl.ds(place(a, q), width), :],
            (((1,), (1,)), ((), ())), preferred_element_type=jnp.float32,
        ).astype(jnp.bfloat16)

    whiten_chunk(1)
    pl.semaphore_wait(barrier, lines + 1)
    halo(0).start()
    halo(1).start()
    launch(first(1))
    w_copy(1, a).start()

    @pl.loop(1, CHUNKS)
    def _(j):
        @pl.when(j == CHUNKS - 2)
        def _():
            halo(0).wait_recv()
            halo(1).wait_recv()
            xt[0:EDGE, :] = jnp.where(a > 0, low[...], 0.0).T
            xt[seg + EDGE : seg + 2 * EDGE, :] = jnp.where(a < peers - 1, high[...], 0.0).T
            split(0)
            split(seg + EDGE)

        whiten_chunk(nth(j))
        launch(first(nth(j)))

        @pl.when(j >= 2)
        def _():
            w_copy(nth(j - 1), a).start()
            to_twin(nth(j - 2), a)

    w_copy(nth(final), a).start()

    @pl.loop(0, 2)
    def _(j):
        fill_partners(nth(j), a)

    near = a * (seg + 256)
    far = other * seg

    def add_chunk(base, q):
        add_terms(w_ref, xp_ref, acc_ref, pl.multiple_of(base + q * width, 256), width)

    @pl.loop(0, CHUNKS)
    def _(j):
        add_chunk(near, jnp.where(j < final - a, final - 1 - a - j, j))

        @pl.when(j == 0)
        def _():
            to_twin(nth(final - 1), a)
            across_time(nth(0))
            across_time(nth(1))
            fill_partners(nth(final - 1), a)

        @pl.when(j == 1)
        def _():
            to_twin(nth(final), a)
            across_time(nth(final - 1))
            to_twin(nth(0), other)
            fill_partners(nth(final), a)

        @pl.when(j == 2)
        def _():
            to_twin(nth(1), other)
            across_time(nth(final))

    to_twin(nth(final - 1), other)

    def arrive(j):
        q = nth(j)
        fill_partners(q, other)
        w_copy(q, other).wait_recv()

    arrive(0)

    @pl.loop(1, CHUNKS)
    def _(j):
        @pl.when(j < final)
        def _():
            arrive(j)

        add_chunk(far, CHUNKS - 1 - j)

        @pl.when(j == 1)
        def _():
            to_twin(nth(final), other)

    arrive(final)
    halo(0).wait_send()
    halo(1).wait_send()

    @pl.loop(0, CHUNKS)
    def _(j):
        q = nth(j)
        w_copy(q, a).wait_send()
        for copy in first(q) + second(q) + third(q, a) + third(q, other):
            copy.wait_send()


def front(x, filters_t, sources, sizes, slot_most):
    chans, seg = x.shape
    peers, lines, subs = sizes
    rows = sources.shape[0] // peers
    total = peers * seg + 256
    dma = pltpu.SemaphoreType.DMA
    vmem = pl.BlockSpec(memory_space=pltpu.VMEM)
    return pl.pallas_call(
        functools.partial(front_kernel, filters_t.shape[0], sizes, slot_most),
        out_shape=(
            jax.ShapeDtypeStruct((total + EDGE, chans), jnp.bfloat16),
            jax.ShapeDtypeStruct((rows, total + LANES), jnp.bfloat16),
            jax.ShapeDtypeStruct(((HALF + 1) * rows, 2 * chans), jnp.float32),
        ),
        in_specs=[pl.BlockSpec(memory_space=pltpu.HBM)] * 3,
        out_specs=(vmem,) * 3,
        scratch_shapes=[
            pltpu.VMEM(filters_t.shape, jnp.float32),
            pltpu.VMEM((1, sources.shape[0]), jnp.int32),
            pltpu.VMEM((chans, seg), jnp.float32),
            *[pltpu.VMEM((seg // 2 + EDGE + 8, chans), jnp.float32)] * 3,
            pltpu.VMEM((filters_t.shape[0] // 2 + 1, chans), jnp.float32),
            pltpu.VMEM((PAIRS + 8, chans), jnp.float32),
            pltpu.VMEM((2 * PAIRS, chans), jnp.float32),
            pltpu.VMEM((seg + 2 * EDGE, chans), jnp.float32),
            pltpu.VMEM((chans, EDGE), jnp.float32),
            pltpu.VMEM((chans, EDGE), jnp.float32),
            pltpu.VMEM((peers, lines, subs, slot_most, seg), jnp.bfloat16),
            pltpu.VMEM((slot_most, chans), jnp.bfloat16),
            pltpu.VMEM((rows, lines * subs * slot_most), jnp.bfloat16),
            dma((CHUNKS,)), dma((2,)), dma((2,)), dma((2,)), dma((CHUNKS,)), dma((CHUNKS,)),
            dma((CHUNKS, 1 + 2 * lines + 2 * (lines - 1))),
            dma((CHUNKS, peers, lines, subs)),
        ],
        compiler_params=pltpu.CompilerParams(
            vmem_limit_bytes=FRONT_LIMIT, collective_id=0, has_side_effects=True
        ),
        name="front",
    )(*(
        pltpu.with_memory_space_constraint(value, pltpu.HBM)
        for value in (x, filters_t, sources.reshape(1, -1))
    ))


def rest_kernel(scale, seg, w_ref, xp_ref, acc_ref, out_ref, stage, sems):
    rows = xp_ref.shape[0]
    chans = w_ref.shape[1]
    far = (1 - lax.axis_index("tm")) * seg
    width = seg // CHUNKS
    last = pl.multiple_of(far + seg - width, 256)
    copies = []
    for n, (group, term) in enumerate(accumulated(w_ref, xp_ref, last, width + 256, groups())):
        start = group[0]
        for i in group:
            here = slice((i - start) * rows, (i - start + 1) * rows)
            held = acc_ref[i * rows : (i + 1) * rows, :] + term[here]
            if i < HALF:
                stage[i] = held[:, 0:chans] * scale
            stage[i + HALF] = held[:, chans:] * scale
        for m, (low, high) in enumerate(
            ((start, min(group[-1] + 1, HALF)), (start + HALF, group[-1] + 1 + HALF))
        ):
            copy = pltpu.make_async_copy(
                stage.at[low:high], out_ref.at[low:high], sems.at[n, m]
            )
            copy.start()
            copies.append(copy)
    for copy in copies:
        copy.wait()


def rest(w_full, partners, terms, seg, scale):
    rows = partners.shape[0]
    chans = w_full.shape[1]
    vmem = pl.BlockSpec(memory_space=pltpu.VMEM)
    return pl.pallas_call(
        functools.partial(rest_kernel, scale, seg),
        out_shape=jax.ShapeDtypeStruct((LAGS, rows, chans), jnp.float32),
        in_specs=[vmem] * 3,
        out_specs=pl.BlockSpec(memory_space=pl.ANY),
        scratch_shapes=[
            pltpu.VMEM((LAGS, rows, chans), jnp.float32),
            pltpu.SemaphoreType.DMA((len(groups()), 2)),
        ],
        compiler_params=pltpu.CompilerParams(vmem_limit_bytes=REST_LIMIT),
        name="rest",
    )(w_full, partners, terms)


def chunk_of(total):
    return max(d for d in range(256, 1025, 256) if total % d == 0)


def corr_kernel(scale, w_ref, slot_ref, sel_ref, out_ref, rhs, xp, acc):
    parts, seg, chans = w_ref.shape
    span = parts * seg
    rows = sel_ref.shape[0]
    total = rhs.shape[0]
    depth = chunk_of(total)
    rhs[span:total, 0:chans] = jnp.zeros((total - span, chans), jnp.bfloat16)
    rhs[0:HALF, chans:] = jnp.zeros((HALF, chans), jnp.bfloat16)
    rhs[span + HALF : total, chans:] = jnp.zeros((total - span - HALF, chans), jnp.bfloat16)
    xp[:, 0:EDGE] = jnp.zeros((rows, EDGE), jnp.bfloat16)
    xp[:, EDGE + span :] = jnp.zeros((rows, xp.shape[1] - EDGE - span), jnp.bfloat16)
    for part in range(parts):
        rhs[part * seg : (part + 1) * seg, 0:chans] = w_ref[part]
        rhs[HALF + part * seg : HALF + (part + 1) * seg, chans:] = w_ref[part]
        xp[:, EDGE + part * seg : EDGE + (part + 1) * seg] = jnp.dot(
            sel_ref[...], slot_ref[part], preferred_element_type=jnp.float32
        ).astype(jnp.bfloat16)
    acc[...] = jnp.zeros_like(acc)

    @pl.loop(0, total // depth)
    def _(kb):
        k0 = pl.multiple_of(kb * depth, 256)
        xw = xp[:, pl.ds(k0, depth + 128)]
        r = rhs[pl.ds(k0, depth), :]
        for g in range((HALF + 1) // GROUP):
            lhs = jnp.concatenate(
                [
                    pltpu.roll(xw, depth + LANES - HALF - i, 1)[:, :depth]
                    for i in range(g * GROUP, (g + 1) * GROUP)
                ],
                axis=0,
            )
            here = slice(g * GROUP * rows, (g + 1) * GROUP * rows)
            acc[here, :] += jnp.dot(lhs, r, preferred_element_type=jnp.float32)

    for i in range(HALF + 1):
        if i < HALF:
            out_ref[i] = acc[i * rows : (i + 1) * rows, 0:chans] * scale
        out_ref[i + HALF] = acc[i * rows : (i + 1) * rows, chans:] * scale


def correlate(w_full, slots, select, scale):
    parts, seg, chans = w_full.shape
    rows = select.shape[0]
    total = parts * seg + 256
    return pl.pallas_call(
        functools.partial(corr_kernel, scale),
        out_shape=jax.ShapeDtypeStruct((LAGS, rows, chans), jnp.float32),
        in_specs=[pl.BlockSpec(memory_space=pltpu.VMEM)] * 3,
        out_specs=pl.BlockSpec(memory_space=pltpu.VMEM),
        scratch_shapes=[
            pltpu.VMEM((total, 2 * chans), jnp.bfloat16),
            pltpu.VMEM((rows, total + 128), jnp.bfloat16),
            pltpu.VMEM(((HALF + 1) * rows, 2 * chans), jnp.float32),
        ],
        compiler_params=pltpu.CompilerParams(vmem_limit_bytes=VMEM_LIMIT),
        name="correlate",
    )(w_full, slots, select)


def routing(sources, chan_dev, wide):
    partner_count = sources.shape[0]
    my_block = lax.axis_index(("chan", "sub"))
    owners = sources // chan_dev
    within = sources % chan_dev
    is_mine = owners == my_block
    chan_ids = jnp.arange(wide, dtype=jnp.int32)
    slot_most = min(chan_dev, partner_count // 8)
    order_ids = jnp.arange(partner_count, dtype=jnp.int32)
    same_owner = owners[:, None] == owners[None, :]
    earlier = order_ids[None, :] < order_ids[:, None]
    rank_in = jnp.sum((same_owner & earlier).astype(jnp.int32), axis=1)
    choose = (
        (rank_in[None, :] == jnp.arange(slot_most, dtype=jnp.int32)[:, None]) & is_mine[None, :]
    ).astype(jnp.bfloat16)
    onehot = (within[:, None] == chan_ids[None, :]).astype(jnp.bfloat16)
    picker = jnp.dot(choose, onehot, preferred_element_type=jnp.float32).astype(jnp.bfloat16)
    return picker, owners * slot_most + rank_in


def on_device(traces, filters, sources):
    chan_dev, seg_len = traces.shape
    time_devs = lax.axis_size("tm")
    lines, subs = lax.axis_size("chan"), lax.axis_size("sub")
    scale = 1.0 / math.sqrt(seg_len * time_devs)
    paired = filters.shape[1] % 32 == 1 and filters.shape[1] < 2 * LANES
    if time_devs == 2 and subs == 2 and chan_dev == LANES and seg_len % (CHUNKS * 256) == 0 and paired:
        slot_most = min(chan_dev, sources.shape[0] // 8)
        w_full, partners, terms = front(
            traces, filters.T, sources, (time_devs, lines, subs), slot_most
        )
        return jnp.transpose(rest(w_full, partners, terms, seg_len, scale), (1, 0, 2))
    wide = -(-chan_dev // LANES) * LANES
    picker, slot_id = routing(sources, chan_dev, wide)
    if wide != chan_dev:
        traces = jnp.pad(traces, ((0, wide - chan_dev), (0, 0)))
        filters = jnp.pad(filters, ((0, wide - chan_dev), (0, 0)))
    rows = slot_id.shape[0] // time_devs
    slot_count = picker.shape[0] * lines * subs
    forward = [(i, i + 1) for i in range(time_devs - 1)]
    backward = [(target, source) for source, target in forward]
    low = lax.ppermute(traces[:, seg_len - EDGE :], "tm", forward)
    high = lax.ppermute(traces[:, :EDGE], "tm", backward)
    w_t, slot_rows = whiten(traces, low, high, filters.T, picker)
    segment = lax.all_gather(slot_rows, ("chan", "sub"), axis=0, tiled=True)
    w_full = lax.all_gather(w_t, "tm", axis=0, tiled=True)
    every = (
        slot_id[:, None] == jnp.arange(slot_count, dtype=jnp.int32)[None, :]
    ).astype(jnp.bfloat16)
    partners = jnp.dot(every, segment, preferred_element_type=jnp.float32).astype(jnp.bfloat16)
    partners = lax.all_to_all(partners, "tm", split_axis=0, concat_axis=1, tiled=True)
    corr = correlate(
        w_full[None], partners[None], jnp.eye(rows, dtype=jnp.bfloat16), scale
    )
    return jnp.transpose(corr, (1, 0, 2))[:, :, :chan_dev]


def solution(mesh):
    return jax.shard_map(
        on_device,
        mesh=mesh,
        in_specs=(
            P(("groups", "chan", "sub"), "tm"),
            P(("groups", "chan", "sub"), None),
            P("groups"),
        ),
        out_specs=P("tm", None, ("groups", "chan", "sub")),
        check_vma=False,
    )
```
